512 devices in a mesh: gz: 128 (over z, y, core), gy: 4 (over x).
Axes of the slice: x: 4, y: 8, z: 8, core: 2. Of those that a mesh axis runs over, the one named last changes fastest.
Arguments:
- level_input: bfloat16 [128, 32, 64, 128], P('gz', 'gy'), may hold values from -6 to 6
- pre_activation: bfloat16 [128, 32, 64, 128], P('gz', 'gy'), may hold values from -6 to 6
- conv_weight: bfloat16 [3, 3, 3, 128, 128], replicated, may hold values from -0.109375 to 0.109375
- down_weight: bfloat16 [2, 2, 2, 128, 256], replicated, may hold values from -0.1875 to 0.1875
- skip_cotangent: bfloat16 [128, 32, 64, 128], P('gz', 'gy'), may hold values from -12 to 12
- deep_cotangent: bfloat16 [64, 16, 32, 256], P(None, 'gy', None, 'gz'), may hold values from -12 to 12
Outputs:
- input_grad: bfloat16 [128, 32, 64, 128], P('gz', 'gy')
- conv_weight_grad: bfloat16 [3, 3, 3, 128, 128], replicated
- down_weight_grad: bfloat16 [2, 2, 2, 128, 256], replicated
The draws below stay inside these ranges and needn't reach their ends.
All inputs are finite; a program needn't handle non-finite values.
Results may differ from the reference program's by a relative error of at most 0.0054.
Values may be sent and summed in bfloat16 or wider, within the bound.
A program may use at most 64 MiB of HBM per device.

```python
import math
import jax
import jax.numpy as jnp
from jax import lax

C2 = 128
C3 = 256
X2 = 64
Z2 = 128
Y2 = 32
Z3 = 64
Y3 = 16
X3 = 32


def rising(count):
    return jnp.exp(jnp.log(3.0) * jnp.arange(count, dtype=jnp.float32) / max(count - 1, 1))


def scaled_draw(key, shape):
    values = jnp.clip(jax.random.normal(key, shape, jnp.float32), -4.0, 4.0)
    return values * rising(shape[0])[:, None, None, None]


def draw_skip_cotangent(key, part):
    return scaled_draw(key, (Z2, Y2, X2, C2)).astype(jnp.bfloat16)


def draw_deep_cotangent(key, part):
    return scaled_draw(jax.random.fold_in(key, 3), (Z3, Y3, X3, C3)).astype(jnp.bfloat16)


def block_scale(stream_key, dims, pieces, least, largest):
    def one(dim, blocks):
        steps = jax.random.uniform(jax.random.fold_in(jax.random.fold_in(stream_key, 6), dim), (blocks,), jnp.float32, least / len(pieces), largest / len(pieces))
        return jnp.repeat(jnp.exp(steps), dims[dim] // blocks).reshape((-1,) + (1,) * (len(dims) - dim - 1))

    gain = one(*pieces[0])
    for cut in pieces[1:]:
        gain = gain * one(*cut)
    return gain


def noise(stream_key, shape, deviation, bound, cuts=(), kind=jnp.bfloat16):
    values = deviation * jax.random.normal(stream_key, shape, jnp.float32)
    if cuts:
        values = values * block_scale(stream_key, shape, cuts, -0.22, 0.18)
    return jnp.clip(values, -bound, bound).astype(kind)


def setup_inputs(seed: int = 0) -> dict:
    keys = jax.random.split(jax.random.key(seed), 7)
    return {
        "level_input": noise(keys[0], (Z2, Y2, X2, C2), 1.0, 6.0, ((0, 128), (1, 4))),
        "pre_activation": noise(keys[1], (Z2, Y2, X2, C2), 1.0, 6.0, ((0, 128), (1, 4))),
        "conv_weight": noise(keys[2], (3, 3, 3, C2, C2), (27 * C2) ** -0.5, 0.109375),
        "down_weight": noise(keys[3], (2, 2, 2, C2, C3), (8 * C2) ** -0.5, 0.1875),
        "skip_cotangent": draw_skip_cotangent(jax.random.fold_in(keys[6], 71), 0),
        "deep_cotangent": draw_deep_cotangent(jax.random.fold_in(keys[6], 71), 0),
    }


def convolve(batched, kernel):
    return lax.conv_general_dilated(batched, kernel, (1, 1, 1), [(1, 1), (1, 1), (1, 1)], dimension_numbers=('NDHWC', 'DHWIO', 'NDHWC'), precision=lax.Precision.HIGHEST)

def reference(level_input, pre_activation, conv_weight, down_weight, skip_cotangent, deep_cotangent):
    weight_down = down_weight.astype(jnp.float32)

    def spread_plane(plane):
        result = jnp.einsum('yxo,abcio->aybxci', plane.astype(jnp.float32), weight_down)
        return result.reshape(2, Y2, X2, C2)
    down_part = lax.map(spread_plane, deep_cotangent).reshape(Z2, Y2, X2, C2)
    hidden_grad = down_part + skip_cotangent.astype(jnp.float32)
    masked_grad = jnp.where(pre_activation > 0, hidden_grad, jnp.zeros_like(hidden_grad)).astype(jnp.bfloat16)
    hidden = jnp.maximum(pre_activation, jnp.zeros_like(pre_activation))
    blocks = hidden.astype(jnp.float32).reshape(Z3, 2, Y3, 2, X3, 2, C2)
    down_sum = jnp.einsum('zaybxci,zyxo->abcio', blocks, deep_cotangent.astype(jnp.float32))
    down_weight_grad = (down_sum / math.sqrt(Z3 * Y3 * X3)).astype(jnp.bfloat16)
    batched = level_input.astype(jnp.float32)[None]
    outputs, pullback = jax.vjp(convolve, batched, conv_weight.astype(jnp.float32))
    input_total, conv_total = pullback(masked_grad.astype(jnp.float32)[None])
    input_grad = input_total[0].astype(jnp.bfloat16)
    conv_weight_grad = (conv_total / math.sqrt(Z2 * Y2 * X2)).astype(jnp.bfloat16)
    return (input_grad, conv_weight_grad, down_weight_grad)
```

```python
import functools
import math

import jax
import jax.numpy as jnp
from jax import lax
from jax.experimental import pallas as pl
from jax.experimental.pallas import tpu as pltpu
from jax.sharding import PartitionSpec as P

MESH = pl.DeviceIdType.MESH
TAPS = 27
ROWS = 64
LANES = 128
BLOCKS = 44
PARTS = (("x", "y", "z", 0, 20), ("y", "x", "z", 20, 12), ("z", "x", "y", 32, 12))


def grid_sides(gz):
    side = math.isqrt(gz // 2)
    return side, side


class Place:
    def __init__(self, sizes):
        self.n = sizes
        gz = lax.axis_index("gz")
        self.gz = gz
        self.at = {
            "z": gz // (2 * sizes["y"]),
            "y": (gz // 2) % sizes["y"],
            "c": gz % 2,
            "x": lax.axis_index("gy"),
        }

    def peer(self, **moved):
        at = dict(self.at, **moved)
        return ((at["z"] * self.n["y"] + at["y"]) * 2 + at["c"], at["x"])

    def ahead(self, axis, step):
        return (self.at[axis] + step) % self.n[axis]

    def behind(self, axis, step):
        return (self.at[axis] + (self.n[axis] - step)) % self.n[axis]

    def steps(self, axis):
        count = self.n[axis]
        return sorted(range(1, count), key=lambda d: -min(d, count - d))


def remote(src, dst, sems, slot, device):
    return pltpu.make_async_remote_copy(
        src_ref=src,
        dst_ref=dst,
        send_sem=sems.at[0, slot],
        recv_sem=sems.at[1, slot],
        device_id=device,
        device_id_type=MESH,
    )


def part_shapes(part, n):
    a1, a2, a3, _, count = part
    rows = ROWS // n["y"]
    cut = count // n["x"]
    piece = (cut, rows, LANES)
    first = (cut, ROWS, LANES) if a1 == "x" else (count, rows, LANES)
    return first, piece


def part_scratch(part, n):
    a1, a2, a3, _, _ = part
    first, piece = part_shapes(part, n)
    return [
        pltpu.VMEM((n[a1],) + first, jnp.bfloat16),
        pltpu.VMEM((n[a1],) + first, jnp.bfloat16),
        pltpu.VMEM((n[a2],) + piece, jnp.float32),
        pltpu.VMEM((n[a2],) + piece, jnp.float32),
        pltpu.VMEM((n[a3],) + piece, jnp.float32),
        pltpu.SemaphoreType.DMA((2, n[a1])),
        pltpu.SemaphoreType.DMA((2, n[a2])),
        pltpu.SemaphoreType.DMA((2, n[a3])),
        pltpu.SemaphoreType.DMA((2, n[a2])),
        pltpu.SemaphoreType.DMA((2, n[a1])),
        pltpu.SemaphoreType.DMA((2, n[a1])),
    ]


PART_REFS = 11


class PartSum:
    def __init__(self, part, place, total, result, refs, scales):
        self.a1, self.a2, self.a3, self.start, self.count = part
        self.place = place
        self.total = total
        self.result = result
        (self.out1, self.in1, self.out2, self.in2, self.all3) = refs[:5]
        (self.s1, self.s2, self.s3, self.g2, self.g1, self.gc) = refs[5:]
        self.rows = ROWS // place.n["y"]
        self.cut = self.count // place.n["x"]
        self.scales = scales
        self.sent = []

    def start_copy(self, copy):
        copy.start()
        self.sent.append(copy)

    def span(self, ref, axes, where):
        blocks = pl.ds(self.start, self.count)
        rows = slice(None)
        for axis in axes:
            if axis == "x":
                blocks = pl.ds(self.start + where["x"] * self.cut, self.cut)
            else:
                rows = pl.ds(pl.multiple_of(where[axis] * self.rows, self.rows), self.rows)
        return ref.at[blocks, rows]

    def scatter1(self):
        place = self.place
        for step in place.steps(self.a1):
            to = place.ahead(self.a1, step)
            self.out1[to] = self.span(self.total, (self.a1,), {self.a1: to})[...].astype(jnp.bfloat16)
            self.start_copy(
                remote(self.out1.at[to], self.in1.at[place.at[self.a1]], self.s1, step, place.peer(**{self.a1: to}))
            )

    def collect(self, held, sems, axis, first):
        place = self.place
        acc = first
        for step in place.steps(axis)[::-1]:
            source = place.behind(axis, step)
            remote(held.at[source], held.at[source], sems, step, place.peer(**{axis: source})).wait_recv()
            acc = acc + held[source].astype(jnp.float32)
        return acc

    def scatter2(self):
        place = self.place
        own = self.span(self.total, (self.a1,), place.at)[...]
        acc = self.collect(self.in1, self.s1, self.a1, own)
        for to in range(place.n[self.a2]):
            if self.a2 == "x":
                self.out2[to] = acc[to * self.cut : (to + 1) * self.cut]
            else:
                self.out2[to] = acc[:, to * self.rows : (to + 1) * self.rows]
        for step in place.steps(self.a2):
            to = place.ahead(self.a2, step)
            self.start_copy(
                remote(self.out2.at[to], self.in2.at[place.at[self.a2]], self.s2, step, place.peer(**{self.a2: to}))
            )

    def exchange3(self):
        place = self.place
        me = place.at[self.a3]
        self.all3[me] = self.collect(self.in2, self.s2, self.a2, self.out2[place.at[self.a2]])
        for step in place.steps(self.a3):
            to = place.ahead(self.a3, step)
            self.start_copy(remote(self.all3.at[me], self.all3.at[me], self.s3, step, place.peer(**{self.a3: to})))

    def gather2(self):
        place = self.place
        for step in place.steps(self.a3)[::-1]:
            source = place.behind(self.a3, step)
            ref = self.all3.at[source]
            remote(ref, ref, self.s3, step, place.peer(**{self.a3: source})).wait_recv()
        acc = self.all3[0]
        for source in range(1, place.n[self.a3]):
            acc = acc + self.all3[source]
        mine = self.span(self.result, (self.a1, self.a2), place.at)
        conv_scale, down_scale = self.scales
        block = self.start + place.at["x"] * self.cut
        for i in range(self.cut):
            scale = jnp.where(block + i < TAPS, jnp.float32(conv_scale), jnp.float32(down_scale))
            mine[i] = (acc[i] / scale).astype(jnp.bfloat16)
        for step in place.steps(self.a2):
            to = place.ahead(self.a2, step)
            self.start_copy(remote(mine, mine, self.g2, step, place.peer(**{self.a2: to})))

    def gather1(self, partner_result):
        place = self.place
        for step in place.steps(self.a2)[::-1]:
            source = place.behind(self.a2, step)
            ref = self.span(self.result, (self.a1, self.a2), dict(place.at, **{self.a2: source}))
            remote(ref, ref, self.g2, step, place.peer(**{self.a2: source})).wait_recv()
        mine = self.span(self.result, (self.a1,), place.at)
        for step in place.steps(self.a1):
            to = place.ahead(self.a1, step)
            self.start_copy(remote(mine, mine, self.g1, step, place.peer(**{self.a1: to})))
        self.start_copy(remote(mine, mine, self.gc, 0, place.peer(c=1 - place.at["c"])))

    def gather_core(self):
        place = self.place
        for step in place.steps(self.a1)[::-1]:
            source = place.behind(self.a1, step)
            ref = self.span(self.result, (self.a1,), {self.a1: source})
            remote(ref, ref, self.g1, step, place.peer(**{self.a1: source})).wait_recv()
            self.start_copy(remote(ref, ref, self.gc, step, place.peer(c=1 - place.at["c"])))

    def finish(self, other):
        place = self.place
        for step in [0] + place.steps(self.a1)[::-1]:
            source = place.behind(self.a1, step)
            ref = self.span(other, (self.a1,), {self.a1: source})
            remote(ref, ref, self.gc, step, place.peer(c=1 - place.at["c"])).wait_recv()
        for copy in self.sent:
            copy.wait_send()


def store_results(result, conv_out, down_out, sems):
    copies = []
    for core in range(2):
        copies.append(
            pltpu.make_async_copy(result.at[core, pl.ds(0, TAPS)], conv_out.at[:, core], sems.at[3 * core])
        )
        for half in range(2):
            for_half = result.at[core, pl.ds(TAPS + 8 * half, 8)]
            copies.append(
                pltpu.make_async_copy(
                    for_half, down_out.at[core, :, :, pl.ds(LANES * half, LANES)], sems.at[3 * core + 1 + half]
                )
            )
    for copy in copies:
        copy.start()
    for copy in copies:
        copy.wait()


def sum_kernel(n, scales, conv_ref, down_ref, conv_out, down_out, core_in, total, result, core_sems, out_sems, *refs):
    place = Place(n)
    core = place.at["c"]
    barrier = pltpu.get_barrier_semaphore()
    peers = [place.peer(c=1 - core)]
    for axis in "xyz":
        peers += [place.peer(**{axis: place.ahead(axis, step)}) for step in place.steps(axis)]
    for device in peers:
        pl.semaphore_signal(barrier, inc=1, device_id=device, device_id_type=MESH)
    pl.semaphore_wait(barrier, len(peers))

    swap = remote(conv_ref.at[:, 1 - core], core_in, core_sems, 0, place.peer(c=1 - core))
    swap.start()
    total[pl.ds(TAPS, 16)] = down_ref[...]
    total[TAPS + 16] = jnp.zeros((ROWS, LANES), jnp.float32)
    parts = []
    for i, part in enumerate(PARTS):
        parts.append(PartSum(part, place, total, result.at[core], refs[i * PART_REFS : (i + 1) * PART_REFS], scales))
    parts[2].scatter1()
    swap.wait_recv()
    for tap in range(TAPS):
        total[tap] = conv_ref[tap, core] + core_in[tap]
    parts[1].scatter1()
    parts[0].scatter1()
    for stage in ("scatter2", "exchange3", "gather2"):
        for part in parts[::-1]:
            getattr(part, stage)()
    for part in parts[::-1]:
        part.gather1(None)
    for part in parts[::-1]:
        part.gather_core()
    for part in parts[::-1]:
        part.finish(result.at[1 - core])
    swap.wait_send()
    store_results(result, conv_out, down_out, out_sems)


def sum_all(conv_local, down_local, sizes, scales):
    scratch = [
        pltpu.VMEM((TAPS, ROWS, LANES), jnp.float32),
        pltpu.VMEM((BLOCKS, ROWS, LANES), jnp.float32),
        pltpu.VMEM((2, BLOCKS, ROWS, LANES), jnp.bfloat16),
        pltpu.SemaphoreType.DMA((2, 1)),
        pltpu.SemaphoreType.DMA((6,)),
    ]
    for part in PARTS:
        scratch += part_scratch(part, sizes)
    conv_out, down_out = pl.pallas_call(
        functools.partial(sum_kernel, sizes, scales),
        out_shape=(
            jax.ShapeDtypeStruct((TAPS, 2, ROWS, LANES), jnp.bfloat16),
            jax.ShapeDtypeStruct((2, 8, ROWS, 2 * LANES), jnp.bfloat16),
        ),
        in_specs=[pl.BlockSpec(memory_space=pltpu.VMEM)] * 2,
        out_specs=(pl.BlockSpec(memory_space=pl.ANY), pl.BlockSpec(memory_space=pl.ANY)),
        scratch_shapes=scratch,
        compiler_params=pltpu.CompilerParams(
            collective_id=0, has_side_effects=True, vmem_limit_bytes=56 * 1024 * 1024
        ),
    )(conv_local, down_local)
    return conv_out, down_out


def swapped(array, axis, bit):
    return lax.ppermute(array, axis, [(i, i ^ 1 << bit) for i in range(lax.axis_size(axis))])


def extended(cells, sides, width):
    for axis, dim in sides:
        count = lax.axis_size(axis)
        ends = count - 1
        head = lax.slice_in_dim(cells, 0, width, axis=dim)
        tail = lax.slice_in_dim(cells, cells.shape[dim] - width, cells.shape[dim], axis=dim)
        cells = jnp.concatenate(
            [
                lax.ppermute(tail, axis, [(i, (i + 1) % count) for i in range(ends)]),
                cells,
                lax.ppermute(head, axis, [((i + 1) % count, i) for i in range(ends)]),
            ],
            axis=dim,
        )
    return cells


def per_device(
    level_input, pre_activation, conv_weight, down_weight, skip_cotangent, deep_cotangent
):
    row_count = level_input.shape[1]
    col_count = level_input.shape[2]
    channels = level_input.shape[3]
    plane_count = deep_cotangent.shape[0]
    deep_rows = deep_cotangent.shape[1]
    deep_cols = deep_cotangent.shape[2]
    deep_share = deep_cotangent.shape[3]
    parity = lax.axis_index("gz") % 2
    halved = deep_cotangent.reshape(2 * plane_count, deep_rows // 2, deep_cols, deep_share)
    own_half = lax.all_to_all(halved, "gz", split_axis=0, concat_axis=3, tiled=True)[0]
    pair_half = swapped(own_half, "gz", 0)
    even_plane = parity == 0
    top_half = jnp.where(even_plane, own_half, pair_half)
    low_half = jnp.where(even_plane, pair_half, own_half)
    deep_grad = jnp.concatenate([top_half, low_half], axis=0)
    down_slice = lax.dynamic_index_in_dim(down_weight, parity, 0, keepdims=False)
    down_part = jnp.einsum(
        "yxo,bcio->ybxci", deep_grad, down_slice, preferred_element_type=jnp.float32
    )
    down_part = down_part.reshape(row_count, col_count, channels)
    hidden_grad = down_part + skip_cotangent[0].astype(jnp.float32)
    pre_plane = pre_activation[0]
    masked_grad = jnp.where(pre_plane > 0, hidden_grad, jnp.zeros_like(hidden_grad)).astype(
        jnp.bfloat16
    )
    hidden = jnp.maximum(pre_plane, jnp.zeros_like(pre_plane))
    hidden_blocks = hidden.reshape(row_count // 2, 2, col_count // 2, 2, channels)
    down_local = jnp.einsum(
        "ybxci,yxo->bcio", hidden_blocks, deep_grad, preferred_element_type=jnp.float32
    )
    down_blocks = down_local.reshape(8, ROWS, 2, LANES).transpose(2, 0, 1, 3).reshape(16, ROWS, LANES)
    grad_padded = extended(masked_grad[None], (("gz", 0), ("gy", 1)), 1)
    grad_padded = jnp.pad(grad_padded, ((0, 0), (0, 0), (1, 1), (0, 0)))
    input_padded = extended(level_input, (("gz", 0), ("gy", 1)), 1)
    input_padded = jnp.pad(input_padded, ((0, 0), (0, 0), (1, 1), (0, 0)))
    cell_count = row_count * col_count
    grad_flat = masked_grad.reshape(cell_count, channels)
    input_total = jnp.zeros((cell_count, channels), jnp.float32)
    conv_terms = []
    for kernel_z in range(3):
        grad_patches = jnp.concatenate(
            [
                grad_padded[
                    2 - kernel_z,
                    2 - kernel_y : 2 - kernel_y + row_count,
                    2 - kernel_x : 2 - kernel_x + col_count,
                    :,
                ]
                for kernel_y in range(3)
                for kernel_x in range(3)
            ],
            axis=-1,
        )
        grad_patches = grad_patches.reshape(cell_count, 9 * channels)
        conv_matrix = jnp.swapaxes(conv_weight[kernel_z], 2, 3).reshape(9 * channels, channels)
        input_total = input_total + jnp.dot(
            grad_patches, conv_matrix, preferred_element_type=jnp.float32
        )
        input_patches = jnp.concatenate(
            [
                input_padded[
                    kernel_z, kernel_y : kernel_y + row_count, kernel_x : kernel_x + col_count, :
                ]
                for kernel_y in range(3)
                for kernel_x in range(3)
            ],
            axis=-1,
        )
        input_patches = input_patches.reshape(cell_count, 9 * channels)
        slab_grad = lax.dot_general(
            input_patches, grad_flat, (((0,), (0,)), ((), ())), preferred_element_type=jnp.float32
        )
        slab_grad = slab_grad.reshape(3, 3, channels, channels)
        conv_terms.append(slab_grad)
    conv_local = jnp.stack(conv_terms)
    cell_total = lax.axis_size("gz") * lax.axis_size("gy") * cell_count
    conv_scale = math.sqrt(cell_total)
    down_scale = math.sqrt(cell_total // 8)
    conv_local = conv_local.reshape(TAPS, 2, ROWS, LANES)
    side_z, side_y = grid_sides(lax.axis_size("gz"))
    sizes = {"z": side_z, "y": side_y, "x": lax.axis_size("gy"), "c": 2}
    conv_weight_grad, down_weight_grad = sum_all(conv_local, down_blocks, sizes, (conv_scale, down_scale))
    conv_weight_grad = conv_weight_grad.reshape(3, 3, 3, channels, channels)
    down_weight_grad = down_weight_grad.reshape(2, 2, 2, channels, 2 * channels)
    input_grad = input_total.reshape(1, row_count, col_count, channels).astype(jnp.bfloat16)
    return (input_grad, conv_weight_grad, down_weight_grad)


def solution(mesh):
    return jax.shard_map(
        per_device,
        mesh=mesh,
        in_specs=(
            P("gz", "gy", None, None),
            P("gz", "gy", None, None),
            P(),
            P(),
            P("gz", "gy", None, None),
            P(None, "gy", None, "gz"),
        ),
        out_specs=(P("gz", "gy", None, None), P(), P()),
        check_vma=False,
    )
```

```python
import functools
import math

import jax
import jax.numpy as jnp
from jax import lax
from jax.experimental import pallas as pl
from jax.experimental.pallas import tpu as pltpu
from jax.sharding import PartitionSpec as P

MESH = pl.DeviceIdType.MESH
TAPS = 27
ROWS = 64
LANES = 128
BLOCKS = 44
PARTS = (("x", "y", "z", 0, 20), ("y", "x", "z", 20, 12), ("z", "x", "y", 32, 12))


def grid_sides(gz):
    side = math.isqrt(gz // 2)
    return side, side


class Place:
    def __init__(self, sizes):
        self.n = sizes
        gz = lax.axis_index("gz")
        self.gz = gz
        self.at = {
            "z": gz // (2 * sizes["y"]),
            "y": (gz // 2) % sizes["y"],
            "c": gz % 2,
            "x": lax.axis_index("gy"),
        }

    def peer(self, **moved):
        at = dict(self.at, **moved)
        return ((at["z"] * self.n["y"] + at["y"]) * 2 + at["c"], at["x"])

    def ahead(self, axis, step):
        return (self.at[axis] + step) % self.n[axis]

    def behind(self, axis, step):
        return (self.at[axis] + (self.n[axis] - step)) % self.n[axis]

    def steps(self, axis):
        count = self.n[axis]
        return sorted(range(1, count), key=lambda d: -min(d, count - d))


def remote(src, dst, sems, slot, device):
    return pltpu.make_async_remote_copy(
        src_ref=src,
        dst_ref=dst,
        send_sem=sems.at[0, slot],
        recv_sem=sems.at[1, slot],
        device_id=device,
        device_id_type=MESH,
    )


def part_shapes(part, n):
    a1, a2, a3, _, count = part
    rows = ROWS // n["y"]
    cut = count // n["x"]
    piece = (cut, rows, LANES)
    first = (cut, ROWS, LANES) if a1 == "x" else (count, rows, LANES)
    return first, piece


def part_scratch(part, n):
    a1, a2, a3, _, _ = part
    first, piece = part_shapes(part, n)
    return [
        pltpu.VMEM((n[a1],) + first, jnp.bfloat16),
        pltpu.VMEM((n[a1],) + first, jnp.bfloat16),
        pltpu.VMEM((n[a2],) + piece, jnp.float32),
        pltpu.VMEM((n[a2],) + piece, jnp.float32),
        pltpu.VMEM((n[a3],) + piece, jnp.float32),
        pltpu.SemaphoreType.DMA((2, n[a1])),
        pltpu.SemaphoreType.DMA((2, n[a2])),
        pltpu.SemaphoreType.DMA((2, n[a3])),
        pltpu.SemaphoreType.DMA((2, n[a2])),
        pltpu.SemaphoreType.DMA((2, n[a1])),
        pltpu.SemaphoreType.DMA((2, n[a1])),
    ]


PART_REFS = 11


class PartSum:
    def __init__(self, part, place, total, result, refs, scales):
        self.a1, self.a2, self.a3, self.start, self.count = part
        self.place = place
        self.total = total
        self.result = result
        (self.out1, self.in1, self.out2, self.in2, self.all3) = refs[:5]
        (self.s1, self.s2, self.s3, self.g2, self.g1, self.gc) = refs[5:]
        self.rows = ROWS // place.n["y"]
        self.cut = self.count // place.n["x"]
        self.scales = scales
        self.sent = []

    def start_copy(self, copy):
        copy.start()
        self.sent.append(copy)

    def span(self, ref, axes, where):
        blocks = pl.ds(self.start, self.count)
        rows = slice(None)
        for axis in axes:
            if axis == "x":
                blocks = pl.ds(self.start + where["x"] * self.cut, self.cut)
            else:
                rows = pl.ds(pl.multiple_of(where[axis] * self.rows, self.rows), self.rows)
        return ref.at[blocks, rows]

    def scatter1(self):
        place = self.place
        for step in place.steps(self.a1):
            to = place.ahead(self.a1, step)
            self.out1[to] = self.span(self.total, (self.a1,), {self.a1: to})[...].astype(jnp.bfloat16)
            self.start_copy(
                remote(self.out1.at[to], self.in1.at[place.at[self.a1]], self.s1, step, place.peer(**{self.a1: to}))
            )

    def collect(self, held, sems, axis, first):
        place = self.place
        acc = first
        for step in place.steps(axis)[::-1]:
            source = place.behind(axis, step)
            remote(held.at[source], held.at[source], sems, step, place.peer(**{axis: source})).wait_recv()
            acc = acc + held[source].astype(jnp.float32)
        return acc

    def scatter2(self):
        place = self.place
        own = self.span(self.total, (self.a1,), place.at)[...]
        acc = self.collect(self.in1, self.s1, self.a1, own)
        for to in range(place.n[self.a2]):
            if self.a2 == "x":
                self.out2[to] = acc[to * self.cut : (to + 1) * self.cut]
            else:
                self.out2[to] = acc[:, to * self.rows : (to + 1) * self.rows]
        for step in place.steps(self.a2):
            to = place.ahead(self.a2, step)
            self.start_copy(
                remote(self.out2.at[to], self.in2.at[place.at[self.a2]], self.s2, step, place.peer(**{self.a2: to}))
            )

    def exchange3(self):
        place = self.place
        me = place.at[self.a3]
        self.all3[me] = self.collect(self.in2, self.s2, self.a2, self.out2[place.at[self.a2]])
        for step in place.steps(self.a3):
            to = place.ahead(self.a3, step)
            self.start_copy(remote(self.all3.at[me], self.all3.at[me], self.s3, step, place.peer(**{self.a3: to})))

    def gather2(self):
        place = self.place
        for step in place.steps(self.a3)[::-1]:
            source = place.behind(self.a3, step)
            ref = self.all3.at[source]
            remote(ref, ref, self.s3, step, place.peer(**{self.a3: source})).wait_recv()
        acc = self.all3[0]
        for source in range(1, place.n[self.a3]):
            acc = acc + self.all3[source]
        mine = self.span(self.result, (self.a1, self.a2), place.at)
        conv_scale, down_scale = self.scales
        block = self.start + place.at["x"] * self.cut
        for i in range(self.cut):
            scale = jnp.where(block + i < TAPS, jnp.float32(conv_scale), jnp.float32(down_scale))
            mine[i] = (acc[i] / scale).astype(jnp.bfloat16)
        for step in place.steps(self.a2):
            to = place.ahead(self.a2, step)
            self.start_copy(remote(mine, mine, self.g2, step, place.peer(**{self.a2: to})))

    def gather1(self, partner_result):
        place = self.place
        for step in place.steps(self.a2)[::-1]:
            source = place.behind(self.a2, step)
            ref = self.span(self.result, (self.a1, self.a2), dict(place.at, **{self.a2: source}))
            remote(ref, ref, self.g2, step, place.peer(**{self.a2: source})).wait_recv()
        mine = self.span(self.result, (self.a1,), place.at)
        for step in place.steps(self.a1):
            to = place.ahead(self.a1, step)
            self.start_copy(remote(mine, mine, self.g1, step, place.peer(**{self.a1: to})))
        self.start_copy(remote(mine, mine, self.gc, 0, place.peer(c=1 - place.at["c"])))

    def gather_core(self):
        place = self.place
        for step in place.steps(self.a1)[::-1]:
            source = place.behind(self.a1, step)
            ref = self.span(self.result, (self.a1,), {self.a1: source})
            remote(ref, ref, self.g1, step, place.peer(**{self.a1: source})).wait_recv()
            self.start_copy(remote(ref, ref, self.gc, step, place.peer(c=1 - place.at["c"])))

    def finish(self, other):
        place = self.place
        for step in [0] + place.steps(self.a1)[::-1]:
            source = place.behind(self.a1, step)
            ref = self.span(other, (self.a1,), {self.a1: source})
            remote(ref, ref, self.gc, step, place.peer(c=1 - place.at["c"])).wait_recv()
        for copy in self.sent:
            copy.wait_send()


def store_results(result, conv_out, down_out, sems):
    copies = []
    for core in range(2):
        copies.append(
            pltpu.make_async_copy(result.at[core, pl.ds(0, TAPS)], conv_out.at[:, core], sems.at[3 * core])
        )
        for half in range(2):
            for_half = result.at[core, pl.ds(TAPS + 8 * half, 8)]
            copies.append(
                pltpu.make_async_copy(
                    for_half, down_out.at[core, :, :, pl.ds(LANES * half, LANES)], sems.at[3 * core + 1 + half]
                )
            )
    for copy in copies:
        copy.start()
    for copy in copies:
        copy.wait()


SIDES = [(dz, dy) for dz in (1, -1, 0) for dy in (0, 1, -1) if (dz, dy) != (0, 0)]


class Halo:
    def __init__(self, place, counts, padded, sems):
        self.place, self.counts, self.padded, self.sems = place, counts, padded, sems

    def has(self, dz, dy):
        z, y = self.place.gz + dz, self.place.at["x"] + dy
        return (z >= 0) & (z < self.counts[0]) & (y >= 0) & (y < self.counts[1])

    def copy(self, i, rows):
        dz, dy = SIDES[i]
        depth = rows.shape[0]
        if dy == 0:
            src, dst = rows, self.padded.at[1 - dz, pl.ds(1, depth)]
        elif dy == 1:
            src, dst = rows.at[pl.ds(depth - 1, 1)], self.padded.at[1 - dz, pl.ds(0, 1)]
        else:
            src, dst = rows.at[pl.ds(0, 1)], self.padded.at[1 - dz, pl.ds(depth + 1, 1)]
        device = (self.place.gz + dz, self.place.at["x"] + dy)
        return remote(src, dst, self.sems, i, device)

    def clear(self):
        depth = self.padded.shape[1] - 2
        for dz, dy in SIDES:
            rows = {0: pl.ds(1, depth), 1: pl.ds(0, 1), -1: pl.ds(depth + 1, 1)}[dy]

            @pl.when(jnp.logical_not(self.has(-dz, -dy)))
            def _():
                window = self.padded.at[1 - dz, rows]
                window[...] = jnp.zeros(window.shape, window.dtype)

    def send(self, rows):
        for i, side in enumerate(SIDES):
            pl.when(self.has(*side))(self.copy(i, rows).start)

    def receive(self, rows):
        for i, (dz, dy) in enumerate(SIDES):
            pl.when(self.has(-dz, -dy))(self.copy(i, rows).wait_recv)

    def finish(self, rows):
        for i, side in enumerate(SIDES):
            pl.when(self.has(*side))(self.copy(i, rows).wait_send)


def contract(a, b, dims):
    return lax.dot_general(a, b, ((dims[:1], dims[1:]), ((), ())), preferred_element_type=jnp.float32)


def shifted(values, column, count):
    size = values.shape[0]
    ahead = jnp.where(column == count - 1, 0.0, pltpu.roll(values, size - 1, 0))
    behind = jnp.where(column == 0, 0.0, pltpu.roll(values, 1, 0))
    return ahead, behind


def bits(value, start, width):
    return lax.shift_right_logical(value, start) & ((1 << width) - 1)


def level_kernel(
    n,
    counts,
    scales,
    level_ref,
    pre_ref,
    weight_ref,
    down_ref,
    skip_ref,
    deep_ref,
    input_out,
    conv_out,
    down_out,
    order,
    deep_in,
    deep_sorted,
    deep_all,
    level_pad,
    grad_pad,
    grad_wide,
    input_sum,
    input_rows,
    conv_local,
    core_in,
    total,
    result,
    deep_sems,
    plane_sems,
    level_sems,
    grad_sems,
    core_sems,
    out_sems,
    *refs,
):
    place = Place(n)
    core = place.at["c"]
    partner = place.peer(c=1 - core)
    rows, cols = level_ref.shape[0], level_ref.shape[1]
    half = rows // 2 * cols
    level_halo = Halo(place, counts, level_pad, level_sems)
    grad_halo = Halo(place, counts, grad_pad, grad_sems)

    barrier = pltpu.get_barrier_semaphore()
    peers = [partner]
    for axis in "xyz":
        peers += [place.peer(**{axis: place.ahead(axis, step)}) for step in place.steps(axis)]
    peers += [place.peer(y=place.ahead("y", step), c=1 - core) for step in place.steps("y")]
    for device in peers:
        pl.semaphore_signal(barrier, inc=1, device_id=device, device_id_type=MESH)
    arrivals = len(peers)
    for dz, dy in SIDES:
        near = level_halo.has(dz, dy)
        arrivals = arrivals + near.astype(jnp.int32)

        @pl.when(near)
        def _():
            device = (place.gz + dz, place.at["x"] + dy)
            pl.semaphore_signal(barrier, inc=1, device_id=device, device_id_type=MESH)

    wide = order.shape[0]
    share_bits = (deep_ref.shape[1] // n["z"]).bit_length() - 1
    y_bits, z_bits = n["y"].bit_length() - 1, n["z"].bit_length() - 1
    row = lax.broadcasted_iota(jnp.int32, (wide, wide), 0)
    col = lax.broadcasted_iota(jnp.int32, (wide, wide), 1)
    low = bits(row, 0, share_bits)
    source = bits(row, share_bits, 1 + y_bits)
    target = bits(row, share_bits + 1 + y_bits, z_bits)
    wanted = ((source << z_bits) + target << share_bits) + low
    order[...] = jnp.where(col == wanted, 1.0, 0.0).astype(jnp.bfloat16)
    level_halo.clear()
    grad_halo.clear()
    level_pad[1, pl.ds(1, rows)] = level_ref[...]
    total[BLOCKS - 1] = jnp.zeros((ROWS, LANES), jnp.float32)
    me_y, me_z = place.at["y"], place.at["z"]
    deep_in[me_y, core] = deep_ref[me_y]
    pl.semaphore_wait(barrier, arrivals)

    sent = []
    first = []
    for step in place.steps("y") + [0]:
        to = place.ahead("y", step)
        for cross in range(2):
            if step == 0 and cross == 0:
                continue
            there = 1 - core if cross else core
            copy = remote(
                deep_ref.at[to], deep_in.at[me_y, core], deep_sems, 2 * step + cross, place.peer(y=to, c=there)
            )
            copy.start()
            sent.append(copy)
            first.append((step, cross))
    level_halo.send(level_ref)
    for step, cross in first[::-1]:
        origin = place.behind("y", step)
        window = deep_in.at[origin, 1 - core if cross else core]
        remote(window, window, deep_sems, 2 * step + cross, partner).wait_recv()
    held = deep_in[...].reshape(wide, half // 2)
    deep_sorted[...] = contract(order[...], held, (1, 0)).astype(jnp.bfloat16).reshape(deep_sorted.shape)
    for step in place.steps("z"):
        to = place.ahead("z", step)
        copy = remote(deep_sorted.at[to], deep_all.at[me_z], plane_sems, step, place.peer(z=to))
        copy.start()
        sent.append(copy)
    deep_all[me_z] = deep_sorted[me_z]
    for step in place.steps("z")[::-1]:
        window = deep_all.at[place.behind("z", step)]
        remote(window, window, plane_sems, step, partner).wait_recv()

    cell = lax.broadcasted_iota(jnp.int32, (half, half // 2), 0)
    deep_cell = lax.broadcasted_iota(jnp.int32, (half, half // 2), 1)
    spread = jnp.where(lax.shift_right_logical(cell, 1) == deep_cell, 1.0, 0.0).astype(jnp.bfloat16)
    deep = deep_all[...].reshape(wide, half // 2)
    covering = contract(spread, deep, (1, 1)).astype(jnp.bfloat16)
    column = lax.broadcasted_iota(jnp.int32, (half, LANES), 0) & (cols - 1)
    odd = (column & 1) == 1
    down = contract(covering, down_ref[core], (1, 1))
    for b in range(2):
        even_part = down[:, 2 * b * LANES : (2 * b + 1) * LANES]
        odd_part = down[:, (2 * b + 1) * LANES : (2 * b + 2) * LANES]
        grad = jnp.where(odd, odd_part, even_part) + skip_ref[:, b].reshape(half, LANES).astype(jnp.float32)
        grad = jnp.where(pre_ref[:, b].reshape(half, LANES) > 0, grad, 0.0)
        ahead, behind = shifted(grad, column, cols)
        for y in range(rows // 2):
            span = slice(y * cols, (y + 1) * cols)
            grad_pad[1, 1 + 2 * y + b] = grad[span].astype(jnp.bfloat16)
            grad_wide[2 * y + b, :, 0:LANES] = ahead[span].astype(jnp.bfloat16)
            grad_wide[2 * y + b, :, LANES : 2 * LANES] = grad[span].astype(jnp.bfloat16)
            grad_wide[2 * y + b, :, 2 * LANES :] = behind[span].astype(jnp.bfloat16)
    own_rows = grad_pad.at[1, pl.ds(1, rows)]
    grad_halo.send(own_rows)

    grads = grad_wide[...].reshape(rows * cols, 3 * LANES)
    swaps = [None] * 3
    for kz in (1, 0, 2):
        if kz == 1:
            level_halo.receive(level_ref)
        for ky in range(3):
            cells = level_pad[kz, pl.ds(ky, rows)].reshape(rows * cols, LANES)
            slab = contract(cells, grads, (0, 0))
            for kx in range(3):
                for part in range(2):
                    conv_local[kz, part, 3 * ky + kx] = slab[
                        part * ROWS : (part + 1) * ROWS, kx * LANES : (kx + 1) * LANES
                    ]
        swaps[kz] = remote(conv_local.at[kz, 1 - core], core_in.at[kz], core_sems, kz, partner)
        swaps[kz].start()
    for b in range(2):
        hidden = jnp.maximum(pre_ref[:, b].reshape(half, LANES).astype(jnp.float32), 0.0)
        pair = jnp.concatenate([jnp.where(odd, 0.0, hidden), jnp.where(odd, hidden, 0.0)], axis=1)
        slab = contract(pair.astype(jnp.bfloat16), covering, (0, 0))
        for c in range(2):
            for part in range(2):
                for side in range(2):
                    total[TAPS + 8 * side + 2 * (2 * b + c) + part] = slab[
                        c * LANES + part * ROWS : c * LANES + (part + 1) * ROWS, side * LANES : (side + 1) * LANES
                    ]

    parts = []
    for i, part in enumerate(PARTS):
        parts.append(PartSum(part, place, total, result.at[core], refs[i * PART_REFS : (i + 1) * PART_REFS], scales))
    parts[2].scatter1()
    for kz in (1, 0, 2):
        swaps[kz].wait_recv()
        for tap in range(9):
            total[9 * kz + tap] = conv_local[kz, core, tap] + core_in[kz, tap]
    parts[1].scatter1()
    parts[0].scatter1()

    grad_halo.receive(own_rows)
    for kz in range(3):
        acc = None
        for ky in range(3):
            cells = grad_pad[2 - kz, pl.ds(2 - ky, rows)].reshape(rows * cols, LANES)
            term = contract(cells, weight_ref[3 * kz + ky], (1, 1))
            acc = term if acc is None else acc + term
        input_sum[...] = acc if kz == 0 else input_sum[...] + acc
    column = lax.broadcasted_iota(jnp.int32, (rows * cols, LANES), 0) & (cols - 1)
    ahead, _ = shifted(input_sum[:, 0:LANES], column, cols)
    _, behind = shifted(input_sum[:, 2 * LANES :], column, cols)
    sums = input_sum[:, LANES : 2 * LANES] + ahead + behind
    input_rows[...] = sums.astype(jnp.bfloat16).reshape(input_rows.shape)
    input_copy = pltpu.make_async_copy(input_rows, input_out, out_sems.at[6])
    input_copy.start()

    for stage in ("scatter2", "exchange3", "gather2"):
        for part in parts[::-1]:
            getattr(part, stage)()
    for part in parts[::-1]:
        part.gather1(None)
    for part in parts[::-1]:
        part.gather_core()
    for part in parts[::-1]:
        part.finish(result.at[1 - core])
    for copy in sent + swaps:
        copy.wait_send()
    level_halo.finish(level_ref)
    grad_halo.finish(own_rows)
    input_copy.wait()
    store_results(result, conv_out, down_out, out_sems)


def per_device(level_input, pre_activation, conv_weight, down_weight, skip_cotangent, deep_cotangent):
    rows, cols, channels = level_input.shape[1:]
    planes, deep_rows, deep_cols, share = deep_cotangent.shape
    counts = (lax.axis_size("gz"), lax.axis_size("gy"))
    side_z, side_y = grid_sides(counts[0])
    n = {"z": side_z, "y": side_y, "x": counts[1], "c": 2}
    cell_count = rows * cols
    cell_total = counts[0] * counts[1] * cell_count
    scales = (math.sqrt(cell_total), math.sqrt(cell_total // 8))
    deep_cells = deep_rows * deep_cols
    wide = counts[0] * share
    messages = deep_cotangent.reshape(side_z, side_y, deep_cells, share).transpose(1, 0, 3, 2)
    messages = messages.reshape(side_y, side_z * share, deep_cells)
    pad = (3, rows + 2, cols, channels)
    scratch = [
        pltpu.VMEM((wide, wide), jnp.bfloat16),
        pltpu.VMEM((side_y, 2, side_z * share, deep_cells), jnp.bfloat16),
        pltpu.VMEM((side_z, side_y * 2 * share, deep_cells), jnp.bfloat16),
        pltpu.VMEM((side_z, side_y * 2 * share, deep_cells), jnp.bfloat16),
        pltpu.VMEM(pad, jnp.bfloat16),
        pltpu.VMEM(pad, jnp.bfloat16),
        pltpu.VMEM((rows, cols, 3 * channels), jnp.bfloat16),
        pltpu.VMEM((cell_count, 3 * channels), jnp.float32),
        pltpu.VMEM((rows, cols, channels), jnp.bfloat16),
        pltpu.VMEM((3, 2, 9, ROWS, LANES), jnp.float32),
        pltpu.VMEM((3, 9, ROWS, LANES), jnp.float32),
        pltpu.VMEM((BLOCKS, ROWS, LANES), jnp.float32),
        pltpu.VMEM((2, BLOCKS, ROWS, LANES), jnp.bfloat16),
        pltpu.SemaphoreType.DMA((2, 2 * side_y)),
        pltpu.SemaphoreType.DMA((2, side_z)),
        pltpu.SemaphoreType.DMA((2, len(SIDES))),
        pltpu.SemaphoreType.DMA((2, len(SIDES))),
        pltpu.SemaphoreType.DMA((2, 3)),
        pltpu.SemaphoreType.DMA((7,)),
    ]
    for part in PARTS:
        scratch += part_scratch(part, n)
    input_grad, conv_grad, down_grad = pl.pallas_call(
        functools.partial(level_kernel, n, counts, scales),
        out_shape=(
            jax.ShapeDtypeStruct((rows, cols, channels), jnp.bfloat16),
            jax.ShapeDtypeStruct((TAPS, 2, ROWS, LANES), jnp.bfloat16),
            jax.ShapeDtypeStruct((2, 8, ROWS, 2 * LANES), jnp.bfloat16),
        ),
        in_specs=[pl.BlockSpec(memory_space=pltpu.VMEM)] * 6,
        out_specs=[pl.BlockSpec(memory_space=pl.ANY)] * 3,
        scratch_shapes=scratch,
        compiler_params=pltpu.CompilerParams(
            collective_id=0, has_side_effects=True, vmem_limit_bytes=56 * 1024 * 1024
        ),
    )(
        level_input.reshape(rows, cols, channels),
        pre_activation.reshape(rows // 2, 2, cols, channels),
        conv_weight.reshape(9, 3 * channels, channels),
        down_weight.reshape(2, 4 * channels, 2 * channels),
        skip_cotangent.reshape(rows // 2, 2, cols, channels),
        messages,
    )
    return (
        input_grad.reshape(1, rows, cols, channels),
        conv_grad.reshape(3, 3, 3, channels, channels),
        down_grad.reshape(2, 2, 2, channels, 2 * channels),
    )


def solution(mesh):
    return jax.shard_map(
        per_device,
        mesh=mesh,
        in_specs=(
            P("gz", "gy", None, None),
            P("gz", "gy", None, None),
            P(),
            P(),
            P("gz", "gy", None, None),
            P(None, "gy", None, "gz"),
        ),
        out_specs=(P("gz", "gy", None, None), P(), P()),
        check_vma=False,
    )
```

```python
import functools
import math

import jax
import jax.numpy as jnp
from jax import lax
from jax.experimental import pallas as pl
from jax.experimental.pallas import tpu as pltpu
from jax.sharding import PartitionSpec as P

MESH = pl.DeviceIdType.MESH
TAPS = 27
ROWS = 64
LANES = 128
BLOCKS = 44
CONV = 28
PARTS = (("x", "y", "z", 0, 16), ("y", "x", "z", 16, 12), ("z", "x", "y", 28, 16))
PLANES = (1, 0, 2)


def grid_sides(gz):
    side = math.isqrt(gz // 2)
    return side, side


class Place:
    def __init__(self, sizes):
        self.n = sizes
        gz = lax.axis_index("gz")
        self.gz = gz
        self.at = {
            "z": gz // (2 * sizes["y"]),
            "y": (gz // 2) % sizes["y"],
            "c": gz % 2,
            "x": lax.axis_index("gy"),
        }

    def peer(self, **moved):
        at = dict(self.at, **moved)
        return ((at["z"] * self.n["y"] + at["y"]) * 2 + at["c"], at["x"])

    def ahead(self, axis, step):
        return (self.at[axis] + step) % self.n[axis]

    def behind(self, axis, step):
        return (self.at[axis] + (self.n[axis] - step)) % self.n[axis]

    def steps(self, axis):
        count = self.n[axis]
        return sorted(range(1, count), key=lambda d: -min(d, count - d))


def remote(src, dst, sems, slot, device):
    return pltpu.make_async_remote_copy(
        src_ref=src,
        dst_ref=dst,
        send_sem=sems.at[0, slot],
        recv_sem=sems.at[1, slot],
        device_id=device,
        device_id_type=MESH,
    )


def part_shapes(part, n):
    a1, a2, a3, _, count = part
    rows = ROWS // n["y"]
    cut = count // n["x"]
    piece = (cut, rows, LANES)
    first = (cut, ROWS, LANES) if a1 == "x" else (count, rows, LANES)
    return first, piece


def part_scratch(part, n):
    a1, a2, a3, _, _ = part
    first, piece = part_shapes(part, n)
    return [
        pltpu.VMEM((n[a1],) + first, jnp.bfloat16),
        pltpu.VMEM((n[a1],) + first, jnp.bfloat16),
        pltpu.VMEM((n[a2],) + piece, jnp.float32),
        pltpu.VMEM((n[a2],) + piece, jnp.float32),
        pltpu.VMEM((n[a3],) + piece, jnp.float32),
        pltpu.SemaphoreType.DMA((2, n[a1])),
        pltpu.SemaphoreType.DMA((2, n[a2])),
        pltpu.SemaphoreType.DMA((2, n[a3])),
        pltpu.SemaphoreType.DMA((2, n[a2])),
        pltpu.SemaphoreType.DMA((2, n[a1])),
        pltpu.SemaphoreType.DMA((2, n[a1])),
    ]


PART_REFS = 11


class PartSum:
    def __init__(self, part, place, total, result, refs, scales):
        self.a1, self.a2, self.a3, self.start, self.count = part
        self.place = place
        self.total = total
        self.result = result
        (self.out1, self.in1, self.out2, self.in2, self.all3) = refs[:5]
        (self.s1, self.s2, self.s3, self.g2, self.g1, self.gc) = refs[5:]
        self.rows = ROWS // place.n["y"]
        self.cut = self.count // place.n["x"]
        self.scales = scales
        self.sent = []

    def start_copy(self, copy):
        copy.start()
        self.sent.append(copy)

    def span(self, ref, axes, where):
        blocks = pl.ds(self.start, self.count)
        rows = slice(None)
        for axis in axes:
            if axis == "x":
                blocks = pl.ds(self.start + where["x"] * self.cut, self.cut)
            else:
                rows = pl.ds(pl.multiple_of(where[axis] * self.rows, self.rows), self.rows)
        return ref.at[blocks, rows]

    def scatter1(self):
        place = self.place
        for step in place.steps(self.a1):
            to = place.ahead(self.a1, step)
            self.out1[to] = self.span(self.total, (self.a1,), {self.a1: to})[...].astype(jnp.bfloat16)
            self.start_copy(
                remote(self.out1.at[to], self.in1.at[place.at[self.a1]], self.s1, step, place.peer(**{self.a1: to}))
            )

    def collect(self, held, sems, axis, first):
        place = self.place
        acc = first
        for step in place.steps(axis)[::-1]:
            source = place.behind(axis, step)
            remote(held.at[source], held.at[source], sems, step, place.peer(**{axis: source})).wait_recv()
            acc = acc + held[source].astype(jnp.float32)
        return acc

    def scatter2(self):
        place = self.place
        own = self.span(self.total, (self.a1,), place.at)[...]
        acc = self.collect(self.in1, self.s1, self.a1, own)
        for to in range(place.n[self.a2]):
            if self.a2 == "x":
                self.out2[to] = acc[to * self.cut : (to + 1) * self.cut]
            else:
                self.out2[to] = acc[:, to * self.rows : (to + 1) * self.rows]
        for step in place.steps(self.a2):
            to = place.ahead(self.a2, step)
            self.start_copy(
                remote(self.out2.at[to], self.in2.at[place.at[self.a2]], self.s2, step, place.peer(**{self.a2: to}))
            )

    def exchange3(self):
        place = self.place
        me = place.at[self.a3]
        self.all3[me] = self.collect(self.in2, self.s2, self.a2, self.out2[place.at[self.a2]])
        for step in place.steps(self.a3):
            to = place.ahead(self.a3, step)
            self.start_copy(remote(self.all3.at[me], self.all3.at[me], self.s3, step, place.peer(**{self.a3: to})))

    def gather2(self):
        place = self.place
        for step in place.steps(self.a3)[::-1]:
            source = place.behind(self.a3, step)
            ref = self.all3.at[source]
            remote(ref, ref, self.s3, step, place.peer(**{self.a3: source})).wait_recv()
        acc = self.all3[0]
        for source in range(1, place.n[self.a3]):
            acc = acc + self.all3[source]
        mine = self.span(self.result, (self.a1, self.a2), place.at)
        conv_scale, down_scale = self.scales
        block = self.start + place.at["x"] * self.cut
        for i in range(self.cut):
            scale = jnp.where(block + i < CONV, jnp.float32(conv_scale), jnp.float32(down_scale))
            mine[i] = (acc[i] / scale).astype(jnp.bfloat16)
        for step in place.steps(self.a2):
            to = place.ahead(self.a2, step)
            self.start_copy(remote(mine, mine, self.g2, step, place.peer(**{self.a2: to})))

    def gather1(self, partner_result):
        place = self.place
        for step in place.steps(self.a2)[::-1]:
            source = place.behind(self.a2, step)
            ref = self.span(self.result, (self.a1, self.a2), dict(place.at, **{self.a2: source}))
            remote(ref, ref, self.g2, step, place.peer(**{self.a2: source})).wait_recv()
        mine = self.span(self.result, (self.a1,), place.at)
        for step in place.steps(self.a1):
            to = place.ahead(self.a1, step)
            self.start_copy(remote(mine, mine, self.g1, step, place.peer(**{self.a1: to})))
        self.start_copy(remote(mine, mine, self.gc, 0, place.peer(c=1 - place.at["c"])))

    def gather_core(self):
        place = self.place
        for step in place.steps(self.a1)[::-1]:
            source = place.behind(self.a1, step)
            ref = self.span(self.result, (self.a1,), {self.a1: source})
            remote(ref, ref, self.g1, step, place.peer(**{self.a1: source})).wait_recv()
            self.start_copy(remote(ref, ref, self.gc, step, place.peer(c=1 - place.at["c"])))

    def finish(self, other):
        place = self.place
        for step in [0] + place.steps(self.a1)[::-1]:
            source = place.behind(self.a1, step)
            ref = self.span(other, (self.a1,), {self.a1: source})
            remote(ref, ref, self.gc, step, place.peer(c=1 - place.at["c"])).wait_recv()
        for copy in self.sent:
            copy.wait_send()


def store_kernel(rows_ref, result, input_out, conv_out, down_out, sems):
    copies = [pltpu.make_async_copy(rows_ref, input_out, sems.at[0])]
    for core in range(2):
        for place, kz in enumerate(PLANES):
            source = result.at[core, pl.ds(9 * place, 9)]
            copies.append(
                pltpu.make_async_copy(source, conv_out.at[pl.ds(9 * kz, 9), core], sems.at[len(copies)])
            )
        for side in range(2):
            source = result.at[core, pl.ds(CONV + 8 * side, 8)]
            target = down_out.at[core, :, :, pl.ds(LANES * side, LANES)]
            copies.append(pltpu.make_async_copy(source, target, sems.at[len(copies)]))
    for copy in copies:
        copy.start()
    for copy in copies:
        copy.wait()


SIDES = [(dz, dy) for dz in (1, -1, 0) for dy in (0, 1, -1) if (dz, dy) != (0, 0)]


class Halo:
    def __init__(self, place, counts, padded, sems):
        self.place, self.counts, self.padded, self.sems = place, counts, padded, sems

    def has(self, dz, dy):
        z, y = self.place.gz + dz, self.place.at["x"] + dy
        return (z >= 0) & (z < self.counts[0]) & (y >= 0) & (y < self.counts[1])

    def copy(self, i, rows):
        dz, dy = SIDES[i]
        depth = rows.shape[0]
        if dy == 0:
            src, dst = rows, self.padded.at[1 - dz, pl.ds(1, depth)]
        elif dy == 1:
            src, dst = rows.at[pl.ds(depth - 1, 1)], self.padded.at[1 - dz, pl.ds(0, 1)]
        else:
            src, dst = rows.at[pl.ds(0, 1)], self.padded.at[1 - dz, pl.ds(depth + 1, 1)]
        device = (self.place.gz + dz, self.place.at["x"] + dy)
        return remote(src, dst, self.sems, i, device)

    def clear(self):
        depth = self.padded.shape[1] - 2
        for dz, dy in SIDES:
            rows = {0: pl.ds(1, depth), 1: pl.ds(0, 1), -1: pl.ds(depth + 1, 1)}[dy]

            @pl.when(jnp.logical_not(self.has(-dz, -dy)))
            def _():
                window = self.padded.at[1 - dz, rows]
                window[...] = jnp.zeros(window.shape, window.dtype)

    def send(self, rows):
        for i, side in enumerate(SIDES):
            pl.when(self.has(*side))(self.copy(i, rows).start)

    def receive(self, rows):
        for i, (dz, dy) in enumerate(SIDES):
            pl.when(self.has(-dz, -dy))(self.copy(i, rows).wait_recv)

    def finish(self, rows):
        for i, side in enumerate(SIDES):
            pl.when(self.has(*side))(self.copy(i, rows).wait_send)


def contract(a, b, dims):
    return lax.dot_general(a, b, ((dims[:1], dims[1:]), ((), ())), preferred_element_type=jnp.float32)


def shifted(values, column, count):
    size = values.shape[0]
    ahead = jnp.where(column == count - 1, 0.0, pltpu.roll(values, size - 1, 0))
    behind = jnp.where(column == 0, 0.0, pltpu.roll(values, 1, 0))
    return ahead, behind


def bits(value, start, width):
    return lax.shift_right_logical(value, start) & ((1 << width) - 1)


def level_kernel(
    n,
    counts,
    scales,
    level_hbm,
    pre_hbm,
    weight_hbm,
    down_hbm,
    skip_hbm,
    deep_hbm,
    input_rows,
    result,
    pre_ref,
    weight_ref,
    down_ref,
    skip_ref,
    deep_ref,
    deep_out,
    order,
    deep_in,
    deep_sorted,
    deep_all,
    level_pad,
    grad_pad,
    grad_wide,
    input_sum,
    conv_local,
    core_in,
    total,
    load_sems,
    deep_sems,
    plane_sems,
    level_sems,
    grad_sems,
    core_sems,
    *refs,
):
    place = Place(n)
    core = place.at["c"]
    partner = place.peer(c=1 - core)
    rows, cols = level_hbm.shape[0], level_hbm.shape[1]
    half = rows // 2 * cols
    level_halo = Halo(place, counts, level_pad, level_sems)
    grad_halo = Halo(place, counts, grad_pad, grad_sems)

    barrier = pltpu.get_barrier_semaphore()
    peers = [partner]
    for axis in "xyz":
        peers += [place.peer(**{axis: place.ahead(axis, step)}) for step in place.steps(axis)]
    peers += [place.peer(y=place.ahead("y", step), c=1 - core) for step in place.steps("y")]
    for device in peers:
        pl.semaphore_signal(barrier, inc=1, device_id=device, device_id_type=MESH)
    arrivals = len(peers)
    for dz, dy in SIDES:
        near = level_halo.has(dz, dy)
        arrivals = arrivals + near.astype(jnp.int32)

        @pl.when(near)
        def _():
            device = (place.gz + dz, place.at["x"] + dy)
            pl.semaphore_signal(barrier, inc=1, device_id=device, device_id_type=MESH)

    level_ref = level_pad.at[1, pl.ds(1, rows)]
    loads = []
    for i, (source, target) in enumerate(
        (
            (deep_hbm, deep_ref),
            (level_hbm, level_ref),
            (down_hbm.at[core], down_ref),
            (pre_hbm, pre_ref),
            (skip_hbm, skip_ref),
            (weight_hbm, weight_ref),
        )
    ):
        loads.append(pltpu.make_async_copy(source, target, load_sems.at[i]))
        loads[-1].start()

    wide = order.shape[0]
    share, deep_planes = deep_ref.shape[1], deep_ref.shape[2]
    share_bits = share.bit_length() - 1
    y_bits, z_bits = n["y"].bit_length() - 1, n["z"].bit_length() - 1
    row = lax.broadcasted_iota(jnp.int32, (wide, wide), 0)
    col = lax.broadcasted_iota(jnp.int32, (wide, wide), 1)
    low = bits(row, 0, share_bits)
    source = bits(row, share_bits, 1 + y_bits)
    target = bits(row, share_bits + 1 + y_bits, z_bits)
    wanted = ((source << z_bits) + target << share_bits) + low
    order[...] = jnp.where(col == wanted, 1.0, 0.0).astype(jnp.bfloat16)
    level_halo.clear()
    grad_halo.clear()
    total[CONV - 1] = jnp.zeros((ROWS, LANES), jnp.float32)
    me_y, me_z = place.at["y"], place.at["z"]

    message = lax.broadcasted_iota(jnp.int32, (deep_planes * share, deep_planes), 0)
    plane = lax.broadcasted_iota(jnp.int32, (deep_planes * share, deep_planes), 1)
    plane_of = (bits(message, share_bits, z_bits) << y_bits) + bits(message, share_bits + z_bits, y_bits)
    channel_of = bits(message, 0, share_bits)
    loads[0].wait()
    cells = deep_ref[...].astype(jnp.float32)
    packed = None
    for channel in range(share):
        chosen = jnp.where((plane == plane_of) & (channel_of == channel), 1.0, 0.0).astype(jnp.bfloat16)
        term = contract(chosen, cells[:, channel].astype(jnp.bfloat16), (1, 1))
        packed = term if packed is None else packed + term
    deep_out[...] = packed.astype(jnp.bfloat16).reshape(deep_out.shape)
    deep_in[me_y, core] = deep_out[me_y]
    loads[1].wait()
    pl.semaphore_wait(barrier, arrivals)

    sent = []
    first = []
    for step in place.steps("y") + [0]:
        to = place.ahead("y", step)
        for cross in range(2):
            if step == 0 and cross == 0:
                continue
            there = 1 - core if cross else core
            copy = remote(
                deep_out.at[to], deep_in.at[me_y, core], deep_sems, 2 * step + cross, place.peer(y=to, c=there)
            )
            copy.start()
            sent.append(copy)
            first.append((step, cross))
    level_halo.send(level_ref)
    for step, cross in first[::-1]:
        origin = place.behind("y", step)
        window = deep_in.at[origin, 1 - core if cross else core]
        remote(window, window, deep_sems, 2 * step + cross, partner).wait_recv()
    held = deep_in[...].reshape(wide, half // 2)
    deep_sorted[...] = contract(order[...], held, (1, 0)).astype(jnp.bfloat16).reshape(deep_sorted.shape)
    for step in place.steps("z"):
        to = place.ahead("z", step)
        copy = remote(deep_sorted.at[to], deep_all.at[me_z], plane_sems, step, place.peer(z=to))
        copy.start()
        sent.append(copy)
    deep_all[me_z] = deep_sorted[me_z]
    for step in place.steps("z")[::-1]:
        window = deep_all.at[place.behind("z", step)]
        remote(window, window, plane_sems, step, partner).wait_recv()

    cell = lax.broadcasted_iota(jnp.int32, (half, half // 2), 0)
    deep_cell = lax.broadcasted_iota(jnp.int32, (half, half // 2), 1)
    spread = jnp.where(lax.shift_right_logical(cell, 1) == deep_cell, 1.0, 0.0).astype(jnp.bfloat16)
    deep = deep_all[...].reshape(wide, half // 2)
    covering = contract(spread, deep, (1, 1)).astype(jnp.bfloat16)
    column = lax.broadcasted_iota(jnp.int32, (half, LANES), 0) & (cols - 1)
    odd = (column & 1) == 1
    loads[3].wait()
    for b in range(2):
        hidden = jnp.maximum(pre_ref[:, b].reshape(half, LANES).astype(jnp.float32), 0.0)
        pair = jnp.concatenate([jnp.where(odd, 0.0, hidden), jnp.where(odd, hidden, 0.0)], axis=1)
        slab = contract(pair.astype(jnp.bfloat16), covering, (0, 0))
        for c in range(2):
            for part in range(2):
                for side in range(2):
                    total[CONV + 8 * side + 2 * (2 * b + c) + part] = slab[
                        c * LANES + part * ROWS : c * LANES + (part + 1) * ROWS, side * LANES : (side + 1) * LANES
                    ]

    parts = []
    for i, part in enumerate(PARTS):
        parts.append(PartSum(part, place, total, result.at[core], refs[i * PART_REFS : (i + 1) * PART_REFS], scales))
    parts[2].scatter1()

    loads[2].wait()
    loads[4].wait()
    down = contract(covering, down_ref[...], (1, 1))
    for b in range(2):
        even_part = down[:, 2 * b * LANES : (2 * b + 1) * LANES]
        odd_part = down[:, (2 * b + 1) * LANES : (2 * b + 2) * LANES]
        grad = jnp.where(odd, odd_part, even_part) + skip_ref[:, b].reshape(half, LANES).astype(jnp.float32)
        grad = jnp.where(pre_ref[:, b].reshape(half, LANES) > 0, grad, 0.0)
        ahead, behind = shifted(grad, column, cols)
        for y in range(rows // 2):
            span = slice(y * cols, (y + 1) * cols)
            grad_pad[1, 1 + 2 * y + b] = grad[span].astype(jnp.bfloat16)
            grad_wide[2 * y + b, :, 0:LANES] = ahead[span].astype(jnp.bfloat16)
            grad_wide[2 * y + b, :, LANES : 2 * LANES] = grad[span].astype(jnp.bfloat16)
            grad_wide[2 * y + b, :, 2 * LANES :] = behind[span].astype(jnp.bfloat16)
    own_rows = grad_pad.at[1, pl.ds(1, rows)]
    grad_halo.send(own_rows)

    grads = grad_wide[...].reshape(rows * cols, 3 * LANES)
    swaps = [None] * 3
    for kz in PLANES:
        if kz == 1:
            level_halo.receive(level_ref)
        for ky in range(3):
            cells = level_pad[kz, pl.ds(ky, rows)].reshape(rows * cols, LANES)
            slab = contract(cells, grads, (0, 0))
            for kx in range(3):
                for part in range(2):
                    conv_local[kz, part, 3 * ky + kx] = slab[
                        part * ROWS : (part + 1) * ROWS, kx * LANES : (kx + 1) * LANES
                    ]
        swaps[kz] = remote(conv_local.at[kz, 1 - core], core_in.at[kz], core_sems, kz, partner)
        swaps[kz].start()
    for position, kz in enumerate(PLANES):
        swaps[kz].wait_recv()
        for tap in range(9):
            total[9 * position + tap] = conv_local[kz, core, tap] + core_in[kz, tap]
        if position == 1:
            parts[0].scatter1()
    parts[1].scatter1()

    grad_halo.receive(own_rows)
    loads[5].wait()
    for kz in range(3):
        acc = None
        for ky in range(3):
            cells = grad_pad[2 - kz, pl.ds(2 - ky, rows)].reshape(rows * cols, LANES)
            term = contract(cells, weight_ref[3 * kz + ky], (1, 1))
            acc = term if acc is None else acc + term
        input_sum[...] = acc if kz == 0 else input_sum[...] + acc
    column = lax.broadcasted_iota(jnp.int32, (rows * cols, LANES), 0) & (cols - 1)
    ahead, _ = shifted(input_sum[:, 0:LANES], column, cols)
    _, behind = shifted(input_sum[:, 2 * LANES :], column, cols)
    sums = input_sum[:, LANES : 2 * LANES] + ahead + behind
    input_rows[...] = sums.astype(jnp.bfloat16).reshape(input_rows.shape)

    for stage in ("scatter2", "exchange3", "gather2"):
        for part in parts[::-1]:
            getattr(part, stage)()
    for part in parts[::-1]:
        part.gather1(None)
    for part in parts[::-1]:
        part.gather_core()
    for part in parts[::-1]:
        part.finish(result.at[1 - core])
    for copy in sent + swaps:
        copy.wait_send()
    level_halo.finish(level_ref)
    grad_halo.finish(own_rows)


def vmem_output(shape, dtype):
    return pltpu.VMEM(shape, dtype)


def in_vmem(array):
    return pltpu.with_memory_space_constraint(array, pltpu.VMEM)


def in_hbm(array):
    return pltpu.with_memory_space_constraint(array, pltpu.HBM)


def per_device(level_input, pre_activation, conv_weight, down_weight, skip_cotangent, deep_cotangent):
    rows, cols, channels = level_input.shape[1:]
    planes, deep_rows, deep_cols, share = deep_cotangent.shape
    counts = (lax.axis_size("gz"), lax.axis_size("gy"))
    side_z, side_y = grid_sides(counts[0])
    n = {"z": side_z, "y": side_y, "x": counts[1], "c": 2}
    cell_count = rows * cols
    cell_total = counts[0] * counts[1] * cell_count
    scales = (math.sqrt(cell_total), math.sqrt(cell_total // 8))
    deep_cells = deep_rows * deep_cols
    wide = counts[0] * share
    pad = (3, rows + 2, cols, channels)
    scratch = [
        pltpu.VMEM((rows // 2, 2, cols, channels), jnp.bfloat16),
        pltpu.VMEM((9, 3 * channels, channels), jnp.bfloat16),
        pltpu.VMEM((4 * channels, 2 * channels), jnp.bfloat16),
        pltpu.VMEM((rows // 2, 2, cols, channels), jnp.bfloat16),
        pltpu.VMEM((deep_cells, share, planes), jnp.bfloat16),
        pltpu.VMEM((side_y, side_z * share, deep_cells), jnp.bfloat16),
        pltpu.VMEM((wide, wide), jnp.bfloat16),
        pltpu.VMEM((side_y, 2, side_z * share, deep_cells), jnp.bfloat16),
        pltpu.VMEM((side_z, side_y * 2 * share, deep_cells), jnp.bfloat16),
        pltpu.VMEM((side_z, side_y * 2 * share, deep_cells), jnp.bfloat16),
        pltpu.VMEM(pad, jnp.bfloat16),
        pltpu.VMEM(pad, jnp.bfloat16),
        pltpu.VMEM((rows, cols, 3 * channels), jnp.bfloat16),
        pltpu.VMEM((cell_count, 3 * channels), jnp.float32),
        pltpu.VMEM((3, 2, 9, ROWS, LANES), jnp.float32),
        pltpu.VMEM((3, 9, ROWS, LANES), jnp.float32),
        pltpu.VMEM((BLOCKS, ROWS, LANES), jnp.float32),
        pltpu.SemaphoreType.DMA((6,)),
        pltpu.SemaphoreType.DMA((2, 2 * side_y)),
        pltpu.SemaphoreType.DMA((2, side_z)),
        pltpu.SemaphoreType.DMA((2, len(SIDES))),
        pltpu.SemaphoreType.DMA((2, len(SIDES))),
        pltpu.SemaphoreType.DMA((2, 3)),
    ]
    for part in PARTS:
        scratch += part_scratch(part, n)
    input_rows, result = pl.pallas_call(
        functools.partial(level_kernel, n, counts, scales),
        out_shape=(
            vmem_output((rows, cols, channels), jnp.bfloat16),
            vmem_output((2, BLOCKS, ROWS, LANES), jnp.bfloat16),
        ),
        in_specs=[pl.BlockSpec(memory_space=pltpu.HBM)] * 6,
        out_specs=[pl.BlockSpec(memory_space=pltpu.VMEM)] * 2,
        scratch_shapes=scratch,
        compiler_params=pltpu.CompilerParams(
            collective_id=0, has_side_effects=True, vmem_limit_bytes=50 * 1024 * 1024
        ),
    )(
        in_hbm(level_input.reshape(rows, cols, channels)),
        in_hbm(pre_activation.reshape(rows // 2, 2, cols, channels)),
        in_hbm(conv_weight.reshape(9, 3 * channels, channels)),
        in_hbm(down_weight.reshape(2, 4 * channels, 2 * channels)),
        in_hbm(skip_cotangent.reshape(rows // 2, 2, cols, channels)),
        in_hbm(deep_cotangent.transpose(1, 2, 3, 0).reshape(deep_cells, share, planes)),
    )
    input_grad, conv_grad, down_grad = pl.pallas_call(
        store_kernel,
        out_shape=(
            jax.ShapeDtypeStruct((rows, cols, channels), jnp.bfloat16),
            jax.ShapeDtypeStruct((TAPS, 2, ROWS, LANES), jnp.bfloat16),
            jax.ShapeDtypeStruct((2, 8, ROWS, 2 * LANES), jnp.bfloat16),
        ),
        in_specs=[pl.BlockSpec(memory_space=pltpu.VMEM)] * 2,
        out_specs=[pl.BlockSpec(memory_space=pl.ANY)] * 3,
        scratch_shapes=[pltpu.SemaphoreType.DMA((11,))],
    )(in_vmem(input_rows), in_vmem(result))
    return (
        input_grad.reshape(1, rows, cols, channels),
        conv_grad.reshape(3, 3, 3, channels, channels),
        down_grad.reshape(2, 2, 2, channels, 2 * channels),
    )


def solution(mesh):
    return jax.shard_map(
        per_device,
        mesh=mesh,
        in_specs=(
            P("gz", "gy", None, None),
            P("gz", "gy", None, None),
            P(),
            P(),
            P("gz", "gy", None, None),
            P(None, "gy", None, "gz"),
        ),
        out_specs=(P("gz", "gy", None, None), P(), P()),
        check_vma=False,
    )
```

```python
import functools
import math

import jax
import jax.numpy as jnp
from jax import lax
from jax.experimental import pallas as pl
from jax.experimental.pallas import tpu as pltpu
from jax.sharding import PartitionSpec as P

MESH = pl.DeviceIdType.MESH
TAPS = 27
ROWS = 64
LANES = 128
BLOCKS = 44
CONV = 28
PARTS = (
    ("x", "y", "z", 0, 8),
    ("x", "z", "y", 8, 8),
    ("y", "x", "z", 16, 12),
    ("x", "z", "y", 28, 4),
    ("z", "x", "y", 32, 12),
)
ORDER = (4, 3, 0, 1, 2)
PLANES = (1, 0, 2)


def grid_sides(gz):
    side = math.isqrt(gz // 2)
    return side, side


class Place:
    def __init__(self, sizes):
        self.n = sizes
        gz = lax.axis_index("gz")
        self.gz = gz
        self.at = {
            "z": gz // (2 * sizes["y"]),
            "y": (gz // 2) % sizes["y"],
            "c": gz % 2,
            "x": lax.axis_index("gy"),
        }

    def peer(self, **moved):
        at = dict(self.at, **moved)
        return ((at["z"] * self.n["y"] + at["y"]) * 2 + at["c"], at["x"])

    def ahead(self, axis, step):
        return (self.at[axis] + step) % self.n[axis]

    def behind(self, axis, step):
        return (self.at[axis] + (self.n[axis] - step)) % self.n[axis]

    def steps(self, axis):
        count = self.n[axis]
        return sorted(range(1, count), key=lambda d: -min(d, count - d))


def remote(src, dst, sems, slot, device):
    return pltpu.make_async_remote_copy(
        src_ref=src,
        dst_ref=dst,
        send_sem=sems.at[0, slot],
        recv_sem=sems.at[1, slot],
        device_id=device,
        device_id_type=MESH,
    )


def part_shapes(part, n):
    a1, a2, a3, _, count = part
    rows = ROWS // n["y"]
    cut = count // n["x"]
    piece = (cut, rows, LANES)
    first = (cut, ROWS, LANES) if a1 == "x" else (count, rows, LANES)
    return first, piece


def part_scratch(part, n):
    a1, a2, a3, _, _ = part
    first, piece = part_shapes(part, n)
    return [
        pltpu.VMEM((n[a1],) + first, jnp.bfloat16),
        pltpu.VMEM((n[a1],) + first, jnp.bfloat16),
        pltpu.VMEM((n[a2],) + piece, jnp.float32),
        pltpu.VMEM((n[a2],) + piece, jnp.float32),
        pltpu.VMEM((n[a3],) + piece, jnp.bfloat16),
        pltpu.SemaphoreType.DMA((2, n[a1])),
        pltpu.SemaphoreType.DMA((2, n[a2])),
        pltpu.SemaphoreType.DMA((2, n[a3])),
        pltpu.SemaphoreType.DMA((2, n[a2])),
        pltpu.SemaphoreType.DMA((2, n[a1])),
        pltpu.SemaphoreType.DMA((2, n[a1])),
    ]


PART_REFS = 11


class PartSum:
    def __init__(self, part, place, total, result, refs, scales):
        self.a1, self.a2, self.a3, self.start, self.count = part
        self.place = place
        self.total = total
        self.result = result
        (self.out1, self.in1, self.out2, self.in2, self.all3) = refs[:5]
        (self.s1, self.s2, self.s3, self.g2, self.g1, self.gc) = refs[5:]
        self.rows = ROWS // place.n["y"]
        self.cut = self.count // place.n["x"]
        self.scales = scales
        self.sent = []

    def start_copy(self, copy):
        copy.start()
        self.sent.append(copy)

    def span(self, ref, axes, where):
        blocks = pl.ds(self.start, self.count)
        rows = slice(None)
        for axis in axes:
            if axis == "x":
                blocks = pl.ds(self.start + where["x"] * self.cut, self.cut)
            else:
                rows = pl.ds(pl.multiple_of(where[axis] * self.rows, self.rows), self.rows)
        return ref.at[blocks, rows]

    def scatter1(self):
        place = self.place
        for step in place.steps(self.a1):
            to = place.ahead(self.a1, step)
            self.out1[to] = self.span(self.total, (self.a1,), {self.a1: to})[...].astype(jnp.bfloat16)
            self.start_copy(
                remote(self.out1.at[to], self.in1.at[place.at[self.a1]], self.s1, step, place.peer(**{self.a1: to}))
            )

    def collect(self, held, sems, axis, first):
        place = self.place
        acc = first
        for step in place.steps(axis)[::-1]:
            source = place.behind(axis, step)
            remote(held.at[source], held.at[source], sems, step, place.peer(**{axis: source})).wait_recv()
            acc = acc + held[source].astype(jnp.float32)
        return acc

    def scatter2(self):
        place = self.place
        own = self.span(self.total, (self.a1,), place.at)[...]
        acc = self.collect(self.in1, self.s1, self.a1, own)
        for to in range(place.n[self.a2]):
            if self.a2 == "x":
                self.out2[to] = acc[to * self.cut : (to + 1) * self.cut]
            else:
                self.out2[to] = acc[:, to * self.rows : (to + 1) * self.rows]
        for step in place.steps(self.a2):
            to = place.ahead(self.a2, step)
            self.start_copy(
                remote(self.out2.at[to], self.in2.at[place.at[self.a2]], self.s2, step, place.peer(**{self.a2: to}))
            )

    def exchange3(self):
        place = self.place
        me = place.at[self.a3]
        acc = self.collect(self.in2, self.s2, self.a2, self.out2[place.at[self.a2]])
        self.all3[me] = acc.astype(jnp.bfloat16)
        for step in place.steps(self.a3):
            to = place.ahead(self.a3, step)
            self.start_copy(remote(self.all3.at[me], self.all3.at[me], self.s3, step, place.peer(**{self.a3: to})))

    def gather2(self):
        place = self.place
        for step in place.steps(self.a3)[::-1]:
            source = place.behind(self.a3, step)
            ref = self.all3.at[source]
            remote(ref, ref, self.s3, step, place.peer(**{self.a3: source})).wait_recv()
        acc = self.all3[0].astype(jnp.float32)
        for source in range(1, place.n[self.a3]):
            acc = acc + self.all3[source].astype(jnp.float32)
        mine = self.span(self.result, (self.a1, self.a2), place.at)
        conv_scale, down_scale = self.scales
        block = self.start + place.at["x"] * self.cut
        for i in range(self.cut):
            scale = jnp.where(block + i < CONV, jnp.float32(conv_scale), jnp.float32(down_scale))
            mine[i] = (acc[i] / scale).astype(jnp.bfloat16)
        for step in place.steps(self.a2):
            to = place.ahead(self.a2, step)
            self.start_copy(remote(mine, mine, self.g2, step, place.peer(**{self.a2: to})))

    def gather1(self):
        place = self.place
        for step in place.steps(self.a2)[::-1]:
            source = place.behind(self.a2, step)
            ref = self.span(self.result, (self.a1, self.a2), dict(place.at, **{self.a2: source}))
            remote(ref, ref, self.g2, step, place.peer(**{self.a2: source})).wait_recv()
        mine = self.span(self.result, (self.a1,), place.at)
        for step in place.steps(self.a1):
            to = place.ahead(self.a1, step)
            self.start_copy(remote(mine, mine, self.g1, step, place.peer(**{self.a1: to})))
        self.start_copy(remote(mine, mine, self.gc, 0, place.peer(c=1 - place.at["c"])))

    def gather_core(self):
        place = self.place
        for step in place.steps(self.a1)[::-1]:
            source = place.behind(self.a1, step)
            ref = self.span(self.result, (self.a1,), {self.a1: source})
            remote(ref, ref, self.g1, step, place.peer(**{self.a1: source})).wait_recv()
            self.start_copy(remote(ref, ref, self.gc, step, place.peer(c=1 - place.at["c"])))

    def finish(self, other):
        place = self.place
        for step in [0] + place.steps(self.a1)[::-1]:
            source = place.behind(self.a1, step)
            ref = self.span(other, (self.a1,), {self.a1: source})
            remote(ref, ref, self.gc, step, place.peer(c=1 - place.at["c"])).wait_recv()
        for copy in self.sent:
            copy.wait_send()


def store_kernel(rows_ref, result, input_out, conv_out, down_out, sems):
    copies = [pltpu.make_async_copy(rows_ref, input_out, sems.at[0])]
    for core in range(2):
        for place, kz in enumerate(PLANES):
            source = result.at[core, pl.ds(9 * place, 9)]
            copies.append(
                pltpu.make_async_copy(source, conv_out.at[pl.ds(9 * kz, 9), core], sems.at[len(copies)])
            )
        for side in range(2):
            source = result.at[core, pl.ds(CONV + 8 * side, 8)]
            target = down_out.at[core, :, :, pl.ds(LANES * side, LANES)]
            copies.append(pltpu.make_async_copy(source, target, sems.at[len(copies)]))
    for copy in copies:
        copy.start()
    for copy in copies:
        copy.wait()


SIDES = [(dz, dy) for dz in (1, -1, 0) for dy in (0, 1, -1) if (dz, dy) != (0, 0)]


class Halo:
    def __init__(self, place, counts, padded, sems):
        self.place, self.counts, self.padded, self.sems = place, counts, padded, sems

    def has(self, dz, dy):
        z, y = self.place.gz + dz, self.place.at["x"] + dy
        return (z >= 0) & (z < self.counts[0]) & (y >= 0) & (y < self.counts[1])

    def copy(self, i, rows):
        dz, dy = SIDES[i]
        depth = rows.shape[0]
        if dy == 0:
            src, dst = rows, self.padded.at[1 - dz, pl.ds(1, depth)]
        elif dy == 1:
            src, dst = rows.at[pl.ds(depth - 1, 1)], self.padded.at[1 - dz, pl.ds(0, 1)]
        else:
            src, dst = rows.at[pl.ds(0, 1)], self.padded.at[1 - dz, pl.ds(depth + 1, 1)]
        device = (self.place.gz + dz, self.place.at["x"] + dy)
        return remote(src, dst, self.sems, i, device)

    def clear(self):
        depth = self.padded.shape[1] - 2
        for dz, dy in SIDES:
            rows = {0: pl.ds(1, depth), 1: pl.ds(0, 1), -1: pl.ds(depth + 1, 1)}[dy]

            @pl.when(jnp.logical_not(self.has(-dz, -dy)))
            def _():
                window = self.padded.at[1 - dz, rows]
                window[...] = jnp.zeros(window.shape, window.dtype)

    def send(self, rows):
        for i, side in enumerate(SIDES):
            pl.when(self.has(*side))(self.copy(i, rows).start)

    def receive(self, rows):
        for i, (dz, dy) in enumerate(SIDES):
            pl.when(self.has(-dz, -dy))(self.copy(i, rows).wait_recv)

    def finish(self, rows):
        for i, side in enumerate(SIDES):
            pl.when(self.has(*side))(self.copy(i, rows).wait_send)


def contract(a, b, dims):
    return lax.dot_general(a, b, ((dims[:1], dims[1:]), ((), ())), preferred_element_type=jnp.float32)


def shifted(values, column, count):
    size = values.shape[0]
    ahead = jnp.where(column == count - 1, 0.0, pltpu.roll(values, size - 1, 0))
    behind = jnp.where(column == 0, 0.0, pltpu.roll(values, 1, 0))
    return ahead, behind


def bits(value, start, width):
    return lax.shift_right_logical(value, start) & ((1 << width) - 1)


def level_kernel(
    n,
    counts,
    scales,
    level_hbm,
    pre_hbm,
    weight_hbm,
    down_hbm,
    skip_hbm,
    deep_hbm,
    input_rows,
    result,
    pre_ref,
    weight_ref,
    down_ref,
    skip_ref,
    deep_ref,
    deep_out,
    order,
    deep_in,
    deep_sorted,
    deep_all,
    level_pad,
    grad_pad,
    grad_wide,
    hidden_turned,
    level_turned,
    input_sum,
    conv_local,
    core_in,
    total,
    load_sems,
    deep_sems,
    plane_sems,
    level_sems,
    grad_sems,
    core_sems,
    *refs,
):
    place = Place(n)
    core = place.at["c"]
    partner = place.peer(c=1 - core)
    rows, cols = level_hbm.shape[0], level_hbm.shape[1]
    half = rows // 2 * cols
    level_halo = Halo(place, counts, level_pad, level_sems)
    grad_halo = Halo(place, counts, grad_pad, grad_sems)

    barrier = pltpu.get_barrier_semaphore()
    peers = []
    for step in place.steps("y"):
        peers += [place.peer(y=place.ahead("y", step)), place.peer(y=place.ahead("y", step), c=1 - core)]
    peers.append(partner)
    for axis in "zx":
        peers += [place.peer(**{axis: place.ahead(axis, step)}) for step in place.steps(axis)]
    for device in peers:
        pl.semaphore_signal(barrier, inc=1, device_id=device, device_id_type=MESH)
    arrivals = len(peers)
    for dz, dy in SIDES:
        near = level_halo.has(dz, dy)
        arrivals = arrivals + near.astype(jnp.int32)

        @pl.when(near)
        def _():
            device = (place.gz + dz, place.at["x"] + dy)
            pl.semaphore_signal(barrier, inc=1, device_id=device, device_id_type=MESH)

    level_ref = level_pad.at[1, pl.ds(1, rows)]
    loads = []
    for i, (source, target) in enumerate(
        (
            (deep_hbm, deep_ref),
            (level_hbm, level_ref),
            (down_hbm.at[core], down_ref),
            (pre_hbm, pre_ref),
            (skip_hbm, skip_ref),
            (weight_hbm, weight_ref),
        )
    ):
        loads.append(pltpu.make_async_copy(source, target, load_sems.at[i]))
        loads[-1].start()

    wide = order.shape[0]
    share, deep_planes = deep_ref.shape[1], deep_ref.shape[2]
    share_bits = share.bit_length() - 1
    y_bits, z_bits = n["y"].bit_length() - 1, n["z"].bit_length() - 1
    row = lax.broadcasted_iota(jnp.int32, (wide, wide), 0)
    col = lax.broadcasted_iota(jnp.int32, (wide, wide), 1)
    low = bits(row, 0, share_bits)
    source = bits(row, share_bits, 1 + y_bits)
    target = bits(row, share_bits + 1 + y_bits, z_bits)
    wanted = ((source << z_bits) + target << share_bits) + low
    order[...] = jnp.where(col == wanted, 1.0, 0.0).astype(jnp.bfloat16)
    level_halo.clear()
    grad_halo.clear()
    total[CONV - 1] = jnp.zeros((ROWS, LANES), jnp.float32)
    me_y, me_z = place.at["y"], place.at["z"]

    message = lax.broadcasted_iota(jnp.int32, (deep_planes * share, deep_planes), 0)
    plane = lax.broadcasted_iota(jnp.int32, (deep_planes * share, deep_planes), 1)
    plane_of = (bits(message, share_bits, z_bits) << y_bits) + bits(message, share_bits + z_bits, y_bits)
    channel_of = bits(message, 0, share_bits)
    loads[0].wait()
    cells = deep_ref[...].astype(jnp.float32)
    packed = None
    for channel in range(share):
        chosen = jnp.where((plane == plane_of) & (channel_of == channel), 1.0, 0.0).astype(jnp.bfloat16)
        term = contract(chosen, cells[:, channel].astype(jnp.bfloat16), (1, 1))
        packed = term if packed is None else packed + term
    deep_out[...] = packed.astype(jnp.bfloat16).reshape(deep_out.shape)
    deep_in[me_y, core] = deep_out[me_y]
    loads[1].wait()
    pl.semaphore_wait(barrier, arrivals)

    sent = []
    first = []
    for step in place.steps("y") + [0]:
        to = place.ahead("y", step)
        for cross in range(2):
            if step == 0 and cross == 0:
                continue
            there = 1 - core if cross else core
            copy = remote(
                deep_out.at[to], deep_in.at[me_y, core], deep_sems, 2 * step + cross, place.peer(y=to, c=there)
            )
            copy.start()
            sent.append(copy)
            first.append((step, cross))
    level_halo.send(level_ref)
    for step, cross in first[::-1]:
        origin = place.behind("y", step)
        window = deep_in.at[origin, 1 - core if cross else core]
        remote(window, window, deep_sems, 2 * step + cross, partner).wait_recv()
    held = deep_in[...].reshape(wide, half // 2)
    deep_sorted[...] = contract(order[...], held, (1, 0)).astype(jnp.bfloat16).reshape(deep_sorted.shape)
    for step in place.steps("z"):
        to = place.ahead("z", step)
        copy = remote(deep_sorted.at[to], deep_all.at[me_z], plane_sems, step, place.peer(z=to))
        copy.start()
        sent.append(copy)
    deep_all[me_z] = deep_sorted[me_z]

    column = lax.broadcasted_iota(jnp.int32, (half, LANES), 0) & (cols - 1)
    odd = (column & 1) == 1
    loads[3].wait()
    for b in range(2):
        hidden = jnp.maximum(pre_ref[:, b].reshape(half, LANES).astype(jnp.float32), 0.0)
        for c in range(2):
            chosen = jnp.where(odd, hidden, 0.0) if c else jnp.where(odd, 0.0, hidden)
            hidden_turned[b, pl.ds(c * LANES, LANES)] = chosen.astype(jnp.bfloat16).T
    level_halo.receive(level_ref)
    for kz in PLANES:
        for ky in range(3):
            cells = level_pad[kz, pl.ds(ky, rows)].reshape(rows * cols, LANES)
            level_turned[kz, pl.ds(ky * LANES, LANES)] = cells.T
    for step in place.steps("z")[::-1]:
        window = deep_all.at[place.behind("z", step)]
        remote(window, window, plane_sems, step, partner).wait_recv()

    cell = lax.broadcasted_iota(jnp.int32, (half, half // 2), 0)
    deep_cell = lax.broadcasted_iota(jnp.int32, (half, half // 2), 1)
    spread = jnp.where(lax.shift_right_logical(cell, 1) == deep_cell, 1.0, 0.0).astype(jnp.bfloat16)
    deep = deep_all[...].reshape(wide, half // 2)
    covering = contract(spread, deep, (1, 1)).astype(jnp.bfloat16)
    for b in range(2):
        slab = contract(hidden_turned[b], covering, (1, 0))
        for c in range(2):
            for part in range(2):
                for side in range(2):
                    total[CONV + 8 * side + 2 * (2 * b + c) + part] = slab[
                        c * LANES + part * ROWS : c * LANES + (part + 1) * ROWS, side * LANES : (side + 1) * LANES
                    ]

    parts = []
    for i, part in enumerate(PARTS):
        parts.append(PartSum(part, place, total, result.at[core], refs[i * PART_REFS : (i + 1) * PART_REFS], scales))
    parts[4].scatter1()
    parts[3].scatter1()

    loads[2].wait()
    loads[4].wait()
    down = contract(covering, down_ref[...], (1, 1))
    for b in range(2):
        even_part = down[:, 2 * b * LANES : (2 * b + 1) * LANES]
        odd_part = down[:, (2 * b + 1) * LANES : (2 * b + 2) * LANES]
        grad = jnp.where(odd, odd_part, even_part) + skip_ref[:, b].reshape(half, LANES).astype(jnp.float32)
        grad = jnp.where(pre_ref[:, b].reshape(half, LANES) > 0, grad, 0.0)
        ahead, behind = shifted(grad, column, cols)
        for y in range(rows // 2):
            span = slice(y * cols, (y + 1) * cols)
            grad_pad[1, 1 + 2 * y + b] = grad[span].astype(jnp.bfloat16)
            grad_wide[2 * y + b, :, 0:LANES] = ahead[span].astype(jnp.bfloat16)
            grad_wide[2 * y + b, :, LANES : 2 * LANES] = grad[span].astype(jnp.bfloat16)
            grad_wide[2 * y + b, :, 2 * LANES :] = behind[span].astype(jnp.bfloat16)
    own_rows = grad_pad.at[1, pl.ds(1, rows)]
    grad_halo.send(own_rows)

    grads = grad_wide[...].reshape(rows * cols, 3 * LANES)
    swaps = []

    def swapped(position):
        swaps[position].wait_recv()
        kz = PLANES[position]
        for tap in range(9):
            total[9 * position + tap] = conv_local[kz, core, tap] + core_in[kz, tap]

    for position, kz in enumerate(PLANES):
        slab = contract(level_turned[kz], grads, (1, 0))
        for ky in range(3):
            for kx in range(3):
                for part in range(2):
                    conv_local[kz, part, 3 * ky + kx] = slab[
                        ky * LANES + part * ROWS : ky * LANES + (part + 1) * ROWS, kx * LANES : (kx + 1) * LANES
                    ]
        swaps.append(remote(conv_local.at[kz, 1 - core], core_in.at[kz], core_sems, kz, partner))
        swaps[position].start()
        if position:
            swapped(position - 1)
            parts[position - 1].scatter1()
    swapped(2)
    parts[2].scatter1()

    grad_halo.receive(own_rows)
    loads[5].wait()
    for kz in range(3):
        acc = None
        for ky in range(3):
            cells = grad_pad[2 - kz, pl.ds(2 - ky, rows)].reshape(rows * cols, LANES)
            term = contract(cells, weight_ref[3 * kz + ky], (1, 1))
            acc = term if acc is None else acc + term
        input_sum[...] = acc if kz == 0 else input_sum[...] + acc
    column = lax.broadcasted_iota(jnp.int32, (rows * cols, LANES), 0) & (cols - 1)
    ahead, _ = shifted(input_sum[:, 0:LANES], column, cols)
    _, behind = shifted(input_sum[:, 2 * LANES :], column, cols)
    sums = input_sum[:, LANES : 2 * LANES] + ahead + behind
    input_rows[...] = sums.astype(jnp.bfloat16).reshape(input_rows.shape)

    queue = [parts[i] for i in ORDER]
    for stage in ("scatter2", "exchange3", "gather2", "gather1", "gather_core"):
        for part in queue:
            getattr(part, stage)()
    for part in queue:
        part.finish(result.at[1 - core])
    for copy in sent + swaps:
        copy.wait_send()
    level_halo.finish(level_ref)
    grad_halo.finish(own_rows)


def vmem_output(shape, dtype):
    return pltpu.VMEM(shape, dtype)


def in_vmem(array):
    return pltpu.with_memory_space_constraint(array, pltpu.VMEM)


def in_hbm(array):
    return pltpu.with_memory_space_constraint(array, pltpu.HBM)


def per_device(level_input, pre_activation, conv_weight, down_weight, skip_cotangent, deep_cotangent):
    rows, cols, channels = level_input.shape[1:]
    planes, deep_rows, deep_cols, share = deep_cotangent.shape
    counts = (lax.axis_size("gz"), lax.axis_size("gy"))
    side_z, side_y = grid_sides(counts[0])
    n = {"z": side_z, "y": side_y, "x": counts[1], "c": 2}
    cell_count = rows * cols
    cell_total = counts[0] * counts[1] * cell_count
    scales = (math.sqrt(cell_total), math.sqrt(cell_total // 8))
    deep_cells = deep_rows * deep_cols
    wide = counts[0] * share
    pad = (3, rows + 2, cols, channels)
    scratch = [
        pltpu.VMEM((rows // 2, 2, cols, channels), jnp.bfloat16),
        pltpu.VMEM((9, 3 * channels, channels), jnp.bfloat16),
        pltpu.VMEM((4 * channels, 2 * channels), jnp.bfloat16),
        pltpu.VMEM((rows // 2, 2, cols, channels), jnp.bfloat16),
        pltpu.VMEM((deep_cells, share, planes), jnp.bfloat16),
        pltpu.VMEM((side_y, side_z * share, deep_cells), jnp.bfloat16),
        pltpu.VMEM((wide, wide), jnp.bfloat16),
        pltpu.VMEM((side_y, 2, side_z * share, deep_cells), jnp.bfloat16),
        pltpu.VMEM((side_z, side_y * 2 * share, deep_cells), jnp.bfloat16),
        pltpu.VMEM((side_z, side_y * 2 * share, deep_cells), jnp.bfloat16),
        pltpu.VMEM(pad, jnp.bfloat16),
        pltpu.VMEM(pad, jnp.bfloat16),
        pltpu.VMEM((rows, cols, 3 * channels), jnp.bfloat16),
        pltpu.VMEM((2, 2 * channels, cell_count // 2), jnp.bfloat16),
        pltpu.VMEM((3, 3 * channels, cell_count), jnp.bfloat16),
        pltpu.VMEM((cell_count, 3 * channels), jnp.float32),
        pltpu.VMEM((3, 2, 9, ROWS, LANES), jnp.float32),
        pltpu.VMEM((3, 9, ROWS, LANES), jnp.float32),
        pltpu.VMEM((BLOCKS, ROWS, LANES), jnp.float32),
        pltpu.SemaphoreType.DMA((6,)),
        pltpu.SemaphoreType.DMA((2, 2 * side_y)),
        pltpu.SemaphoreType.DMA((2, side_z)),
        pltpu.SemaphoreType.DMA((2, len(SIDES))),
        pltpu.SemaphoreType.DMA((2, len(SIDES))),
        pltpu.SemaphoreType.DMA((2, 3)),
    ]
    for part in PARTS:
        scratch += part_scratch(part, n)
    input_rows, result = pl.pallas_call(
        functools.partial(level_kernel, n, counts, scales),
        out_shape=(
            vmem_output((rows, cols, channels), jnp.bfloat16),
            vmem_output((2, BLOCKS, ROWS, LANES), jnp.bfloat16),
        ),
        in_specs=[pl.BlockSpec(memory_space=pltpu.HBM)] * 6,
        out_specs=[pl.BlockSpec(memory_space=pltpu.VMEM)] * 2,
        scratch_shapes=scratch,
        compiler_params=pltpu.CompilerParams(
            collective_id=0, has_side_effects=True, vmem_limit_bytes=50 * 1024 * 1024
        ),
    )(
        in_hbm(level_input.reshape(rows, cols, channels)),
        in_hbm(pre_activation.reshape(rows // 2, 2, cols, channels)),
        in_hbm(conv_weight.reshape(9, 3 * channels, channels)),
        in_hbm(down_weight.reshape(2, 4 * channels, 2 * channels)),
        in_hbm(skip_cotangent.reshape(rows // 2, 2, cols, channels)),
        in_hbm(deep_cotangent.transpose(1, 2, 3, 0).reshape(deep_cells, share, planes)),
    )
    input_grad, conv_grad, down_grad = pl.pallas_call(
        store_kernel,
        out_shape=(
            jax.ShapeDtypeStruct((rows, cols, channels), jnp.bfloat16),
            jax.ShapeDtypeStruct((TAPS, 2, ROWS, LANES), jnp.bfloat16),
            jax.ShapeDtypeStruct((2, 8, ROWS, 2 * LANES), jnp.bfloat16),
        ),
        in_specs=[pl.BlockSpec(memory_space=pltpu.VMEM)] * 2,
        out_specs=[pl.BlockSpec(memory_space=pl.ANY)] * 3,
        scratch_shapes=[pltpu.SemaphoreType.DMA((11,))],
    )(in_vmem(input_rows), in_vmem(result))
    return (
        input_grad.reshape(1, rows, cols, channels),
        conv_grad.reshape(3, 3, 3, channels, channels),
        down_grad.reshape(2, 2, 2, channels, 2 * channels),
    )


def solution(mesh):
    return jax.shard_map(
        per_device,
        mesh=mesh,
        in_specs=(
            P("gz", "gy", None, None),
            P("gz", "gy", None, None),
            P(),
            P(),
            P("gz", "gy", None, None),
            P(None, "gy", None, "gz"),
        ),
        out_specs=(P("gz", "gy", None, None), P(), P()),
        check_vma=False,
    )
```

```python
import functools
import math

import jax
import jax.numpy as jnp
from jax import lax
from jax.experimental import pallas as pl
from jax.experimental.pallas import tpu as pltpu
from jax.sharding import PartitionSpec as P

MESH = pl.DeviceIdType.MESH
TAPS = 27
ROWS = 64
LANES = 128
BLOCKS = 44
CONV = 28
PARTS = (
    ("x", "y", "z", 0, 8),
    ("x", "z", "y", 8, 8),
    ("x", "y", "z", 16, 4),
    ("y", "x", "z", 20, 8),
    ("x", "z", "y", 28, 4),
    ("z", "x", "y", 32, 12),
)
ORDER = (5, 4, 0, 1, 2, 3)
PLANES = (1, 0, 2)


def grid_sides(gz):
    side = math.isqrt(gz // 2)
    return side, side


class Place:
    def __init__(self, sizes):
        self.n = sizes
        gz = lax.axis_index("gz")
        self.gz = gz
        self.at = {
            "z": gz // (2 * sizes["y"]),
            "y": (gz // 2) % sizes["y"],
            "c": gz % 2,
            "x": lax.axis_index("gy"),
        }

    def peer(self, **moved):
        at = dict(self.at, **moved)
        return ((at["z"] * self.n["y"] + at["y"]) * 2 + at["c"], at["x"])

    def ahead(self, axis, step):
        return (self.at[axis] + step) % self.n[axis]

    def behind(self, axis, step):
        return (self.at[axis] + (self.n[axis] - step)) % self.n[axis]

    def steps(self, axis):
        count = self.n[axis]
        return sorted(range(1, count), key=lambda d: -min(d, count - d))


def remote(src, dst, send_sem, recv_sem, device):
    return pltpu.make_async_remote_copy(
        src_ref=src,
        dst_ref=dst,
        send_sem=send_sem,
        recv_sem=recv_sem,
        device_id=device,
        device_id_type=MESH,
    )


def wait_bytes(window, sem):
    pltpu.make_async_copy(window, window, sem).wait()


def part_shapes(part, n):
    a1, a2, a3, _, count = part
    rows = ROWS // n["y"]
    cut = count // n["x"]
    piece = (cut, rows, LANES)
    first = (cut, ROWS, LANES) if a1 == "x" else (count, rows, LANES)
    return first, piece


def part_rows(part, n):
    a1, a2, a3, _, count = part
    first, piece = (math.prod(shape) // LANES for shape in part_shapes(part, n))
    stages = (n[a1] - 1) * first + (n[a2] - 1) * 2 * piece + (n[a3] - 1) * piece
    return stages + (n[a2] - 1) * piece + (n[a1] - 1) * first + count * ROWS


def part_scratch(part, n):
    a1, a2, a3, _, _ = part
    first, piece = part_shapes(part, n)
    return [
        pltpu.VMEM((n[a1],) + first, jnp.bfloat16),
        pltpu.VMEM((n[a1],) + first, jnp.bfloat16),
        pltpu.VMEM((n[a2],) + piece, jnp.float32),
        pltpu.VMEM((n[a2],) + piece, jnp.float32),
        pltpu.VMEM((n[a3],) + piece, jnp.bfloat16),
        pltpu.SemaphoreType.DMA((7,)),
    ]


PART_REFS = 6


class PartSum:
    def __init__(self, part, place, total, result, refs, scales):
        self.a1, self.a2, self.a3, self.start, self.count = part
        self.part = part
        self.place = place
        self.total = total
        self.result = result
        self.out1, self.in1, self.out2, self.in2, self.all3, self.sems = refs
        self.rows = ROWS // place.n["y"]
        self.cut = self.count // place.n["x"]
        self.scales = scales

    def send(self, src, dst, stage, **moved):
        remote(src, dst, self.sems.at[6], self.sems.at[stage], self.place.peer(**moved)).start()

    def span(self, ref, axes, where, times=1):
        blocks = pl.ds(self.start, self.count)
        rows = slice(None)
        for axis in axes:
            wide = times if axis == axes[-1] else 1
            if axis == "x":
                blocks = pl.ds(self.start + where["x"] * self.cut, self.cut * wide)
            else:
                rows = pl.ds(pl.multiple_of(where[axis] * self.rows, self.rows), self.rows * wide)
        return ref.at[blocks, rows]

    def scatter1(self):
        place = self.place
        for step in place.steps(self.a1):
            to = place.ahead(self.a1, step)
            self.out1[to] = self.span(self.total, (self.a1,), {self.a1: to})[...].astype(jnp.bfloat16)
            self.send(self.out1.at[to], self.in1.at[place.at[self.a1]], 0, **{self.a1: to})

    def collect(self, held, stage, axis, first):
        place = self.place
        wait_bytes(held.at[pl.ds(0, place.n[axis] - 1)], self.sems.at[stage])
        acc = first
        for step in place.steps(axis):
            acc = acc + held[place.behind(axis, step)].astype(jnp.float32)
        return acc

    def scatter2(self):
        place = self.place
        own = self.span(self.total, (self.a1,), place.at)[...]
        acc = self.collect(self.in1, 0, self.a1, own)
        for to in range(place.n[self.a2]):
            if self.a2 == "x":
                self.out2[to] = acc[to * self.cut : (to + 1) * self.cut]
            else:
                self.out2[to] = acc[:, to * self.rows : (to + 1) * self.rows]
        for step in place.steps(self.a2):
            to = place.ahead(self.a2, step)
            self.send(self.out2.at[to], self.in2.at[place.at[self.a2]], 1, **{self.a2: to})

    def exchange3(self):
        place = self.place
        me = place.at[self.a3]
        acc = self.collect(self.in2, 1, self.a2, self.out2[place.at[self.a2]])
        self.all3[me] = acc.astype(jnp.bfloat16)
        for step in place.steps(self.a3):
            self.send(self.all3.at[me], self.all3.at[me], 2, **{self.a3: place.ahead(self.a3, step)})

    def gather2(self):
        place = self.place
        wait_bytes(self.all3.at[pl.ds(0, place.n[self.a3] - 1)], self.sems.at[2])
        acc = self.all3[0].astype(jnp.float32)
        for source in range(1, place.n[self.a3]):
            acc = acc + self.all3[source].astype(jnp.float32)
        mine = self.span(self.result, (self.a1, self.a2), place.at)
        conv_scale, down_scale = self.scales
        scale = down_scale if self.start >= CONV else conv_scale
        mine[...] = (acc / scale).astype(jnp.bfloat16)
        for step in place.steps(self.a2):
            self.send(mine, mine, 3, **{self.a2: place.ahead(self.a2, step)})

    def gather1(self):
        place = self.place
        zero = dict(place.at, **{self.a2: 0})
        wait_bytes(self.span(self.result, (self.a1, self.a2), zero, place.n[self.a2] - 1), self.sems.at[3])
        mine = self.span(self.result, (self.a1,), place.at)
        for step in place.steps(self.a1):
            self.send(mine, mine, 4, **{self.a1: place.ahead(self.a1, step)})
        self.send(mine, mine, 5, c=1 - place.at["c"])

    def gather_core(self):
        place = self.place
        wait_bytes(self.span(self.result, (self.a1,), {self.a1: 0}, place.n[self.a1] - 1), self.sems.at[4])
        for step in place.steps(self.a1):
            ref = self.span(self.result, (self.a1,), {self.a1: place.behind(self.a1, step)})
            self.send(ref, ref, 5, c=1 - place.at["c"])

    def finish(self, other, dummy):
        wait_bytes(other.at[pl.ds(self.start, self.count)], self.sems.at[5])
        wait_bytes(dummy.at[pl.ds(0, part_rows(self.part, self.place.n))], self.sems.at[6])


def store_kernel(rows_ref, result, input_out, conv_out, down_out, sems):
    copies = [pltpu.make_async_copy(rows_ref, input_out, sems.at[0])]
    for core in range(2):
        for place, kz in enumerate(PLANES):
            source = result.at[core, pl.ds(9 * place, 9)]
            copies.append(
                pltpu.make_async_copy(source, conv_out.at[pl.ds(9 * kz, 9), core], sems.at[len(copies)])
            )
        for side in range(2):
            source = result.at[core, pl.ds(CONV + 8 * side, 8)]
            target = down_out.at[core, :, :, pl.ds(LANES * side, LANES)]
            copies.append(pltpu.make_async_copy(source, target, sems.at[len(copies)]))
    for copy in copies:
        copy.start()
    for copy in copies:
        copy.wait()


SIDES = [(dz, dy) for dz in (1, -1, 0) for dy in (0, 1, -1) if (dz, dy) != (0, 0)]


class Halo:
    def __init__(self, place, counts, padded, sems):
        self.place, self.counts, self.padded, self.sems = place, counts, padded, sems
        self.depth = padded.shape[1] - 2

    def neighbour(self, dz, dy):
        z, y = self.counts
        return ((self.place.gz + dz + z) % z, (self.place.at["x"] + dy + y) % y)

    def send(self, sides):
        own = self.padded.at[1, pl.ds(1, self.depth)]
        for dz, dy in sides:
            if dy == 0:
                src, dst = own, self.padded.at[1 - dz, pl.ds(1, self.depth)]
            elif dy == 1:
                src, dst = own.at[pl.ds(self.depth - 1, 1)], self.padded.at[1 - dz, pl.ds(0, 1)]
            else:
                src, dst = own.at[pl.ds(0, 1)], self.padded.at[1 - dz, pl.ds(self.depth + 1, 1)]
            kind = 0 if dy == 0 else 1
            remote(src, dst, self.sems.at[0, kind], self.sems.at[1, kind], self.neighbour(dz, dy)).start()

    def wait(self, way):
        wait_bytes(self.padded.at[pl.ds(0, 2), pl.ds(0, self.depth)], self.sems.at[way, 0])
        wait_bytes(self.padded.at[pl.ds(0, 3), pl.ds(0, 2)], self.sems.at[way, 1])

    def receive(self):
        self.wait(1)
        z, y = self.place.gz, self.place.at["x"]
        everything = slice(None)
        for edge, window in (
            (z == 0, (0, everything)),
            (z == self.counts[0] - 1, (2, everything)),
            (y == 0, (everything, 0)),
            (y == self.counts[1] - 1, (everything, self.depth + 1)),
        ):

            @pl.when(edge)
            def _():
                rows = self.padded.at[window]
                rows[...] = jnp.zeros(rows.shape, rows.dtype)


def contract(a, b, dims):
    return lax.dot_general(a, b, ((dims[:1], dims[1:]), ((), ())), preferred_element_type=jnp.float32)


def shifted(values, column, count):
    size = values.shape[0]
    ahead = jnp.where(column == count - 1, 0.0, pltpu.roll(values, size - 1, 0))
    behind = jnp.where(column == 0, 0.0, pltpu.roll(values, 1, 0))
    return ahead, behind


def bits(value, start, width):
    return lax.shift_right_logical(value, start) & ((1 << width) - 1)


def level_kernel(
    n,
    counts,
    scales,
    level_hbm,
    pre_hbm,
    weight_hbm,
    down_hbm,
    skip_hbm,
    deep_hbm,
    input_rows,
    result,
    pre_ref,
    weight_ref,
    down_ref,
    skip_ref,
    deep_ref,
    deep_out,
    order,
    deep_in,
    deep_sorted,
    deep_all,
    level_pad,
    grad_pad,
    grad_wide,
    hidden_turned,
    level_turned,
    input_sum,
    conv_own,
    conv_out,
    core_in,
    total,
    dummy,
    load_sems,
    deep_sems,
    level_sems,
    grad_sems,
    core_sems,
    *refs,
):
    place = Place(n)
    core = place.at["c"]
    partner = place.peer(c=1 - core)
    rows, cols = level_hbm.shape[0], level_hbm.shape[1]
    half = rows // 2 * cols
    level_halo = Halo(place, counts, level_pad, level_sems)
    grad_halo = Halo(place, counts, grad_pad, grad_sems)

    barrier = pltpu.get_barrier_semaphore()
    peers = []
    for step in place.steps("y"):
        peers += [place.peer(y=place.ahead("y", step)), place.peer(y=place.ahead("y", step), c=1 - core)]
    peers.append(partner)
    for axis in "zx":
        peers += [place.peer(**{axis: place.ahead(axis, step)}) for step in place.steps(axis)]
    peers += [level_halo.neighbour(dz, dy) for dz, dy in SIDES if dz]
    for device in peers:
        pl.semaphore_signal(barrier, inc=1, device_id=device, device_id_type=MESH)
    level_ref = level_pad.at[1, pl.ds(1, rows)]
    loads = []
    for i, (source, target) in enumerate(
        (
            (deep_hbm, deep_ref),
            (level_hbm, level_ref),
            (down_hbm.at[core], down_ref),
            (pre_hbm, pre_ref),
            (skip_hbm, skip_ref),
            (weight_hbm, weight_ref),
        )
    ):
        loads.append(pltpu.make_async_copy(source, target, load_sems.at[i]))
        loads[-1].start()

    wide = order.shape[0]
    share, deep_planes = deep_ref.shape[1], deep_ref.shape[2]
    share_bits = share.bit_length() - 1
    y_bits, z_bits = n["y"].bit_length() - 1, n["z"].bit_length() - 1
    me_y, me_z = place.at["y"], place.at["z"]

    message = lax.broadcasted_iota(jnp.int32, (deep_planes * share, deep_planes), 0)
    plane = lax.broadcasted_iota(jnp.int32, (deep_planes * share, deep_planes), 1)
    plane_of = (bits(message, share_bits, z_bits) << y_bits) + bits(message, share_bits + z_bits, y_bits)
    channel_of = bits(message, 0, share_bits)
    loads[0].wait()
    cells = deep_ref[...].astype(jnp.float32)
    packed = None
    for channel in range(share):
        chosen = jnp.where((plane == plane_of) & (channel_of == channel), 1.0, 0.0).astype(jnp.bfloat16)
        term = contract(chosen, cells[:, channel].astype(jnp.bfloat16), (1, 1))
        packed = term if packed is None else packed + term
    deep_out[...] = packed.astype(jnp.bfloat16).reshape(deep_out.shape)
    deep_in[2 * me_y + core] = deep_out[me_y]
    pl.semaphore_wait(barrier, len(peers))

    for step in place.steps("y") + [0]:
        to = place.ahead("y", step)
        for there in (core, 1 - core) if step else (1 - core,):
            remote(
                deep_out.at[to], deep_in.at[2 * me_y + core], deep_sems.at[0], deep_sems.at[1], place.peer(y=to, c=there)
            ).start()
    row = lax.broadcasted_iota(jnp.int32, (wide, wide), 0)
    col = lax.broadcasted_iota(jnp.int32, (wide, wide), 1)
    low = bits(row, 0, share_bits)
    source = bits(row, share_bits, 1 + y_bits)
    target = bits(row, share_bits + 1 + y_bits, z_bits)
    wanted = ((source << z_bits) + target << share_bits) + low
    order[...] = jnp.where(col == wanted, 1.0, 0.0).astype(jnp.bfloat16)
    total[CONV - 1] = jnp.zeros((ROWS, LANES), jnp.float32)
    loads[1].wait()
    messages = deep_in.at[pl.ds(0, 2 * n["y"] - 1)]
    wait_bytes(messages, deep_sems.at[1])
    held = deep_in[...].reshape(wide, half // 2)
    deep_sorted[...] = contract(order[...], held, (1, 0)).astype(jnp.bfloat16).reshape(deep_sorted.shape)
    for step in place.steps("z"):
        to = place.ahead("z", step)
        remote(deep_sorted.at[to], deep_all.at[me_z], deep_sems.at[2], deep_sems.at[3], place.peer(z=to)).start()
    level_halo.send(SIDES)
    deep_all[me_z] = deep_sorted[me_z]

    column = lax.broadcasted_iota(jnp.int32, (half, LANES), 0) & (cols - 1)
    odd = (column & 1) == 1
    loads[3].wait()
    for b in range(2):
        hidden = jnp.maximum(pre_ref[:, b].reshape(half, LANES).astype(jnp.float32), 0.0)
        for c in range(2):
            chosen = jnp.where(odd, hidden, 0.0) if c else jnp.where(odd, 0.0, hidden)
            hidden_turned[b, pl.ds(c * LANES, LANES)] = chosen.astype(jnp.bfloat16).T
    level_halo.receive()
    for kz in PLANES:
        for ky in range(3):
            cells = level_pad[kz, pl.ds(ky, rows)].reshape(rows * cols, LANES)
            level_turned[kz, pl.ds(ky * LANES, LANES)] = cells.T
    planes = deep_all.at[pl.ds(0, n["z"] - 1)]
    wait_bytes(planes, deep_sems.at[3])

    cell = lax.broadcasted_iota(jnp.int32, (half, half // 2), 0)
    deep_cell = lax.broadcasted_iota(jnp.int32, (half, half // 2), 1)
    spread = jnp.where(lax.shift_right_logical(cell, 1) == deep_cell, 1.0, 0.0).astype(jnp.bfloat16)
    deep = deep_all[...].reshape(wide, half // 2)
    covering = contract(spread, deep, (1, 1)).astype(jnp.bfloat16)
    for b in range(2):
        slab = contract(hidden_turned[b], covering, (1, 0))
        for c in range(2):
            for part in range(2):
                for side in range(2):
                    total[CONV + 8 * side + 2 * (2 * b + c) + part] = slab[
                        c * LANES + part * ROWS : c * LANES + (part + 1) * ROWS, side * LANES : (side + 1) * LANES
                    ]

    parts = []
    for i, part in enumerate(PARTS):
        parts.append(PartSum(part, place, total, result.at[core], refs[i * PART_REFS : (i + 1) * PART_REFS], scales))
    parts[5].scatter1()
    parts[4].scatter1()

    loads[2].wait()
    loads[4].wait()
    down = contract(covering, down_ref[...], (1, 1))
    for b in range(2):
        even_part = down[:, 2 * b * LANES : (2 * b + 1) * LANES]
        odd_part = down[:, (2 * b + 1) * LANES : (2 * b + 2) * LANES]
        grad = jnp.where(odd, odd_part, even_part) + skip_ref[:, b].reshape(half, LANES).astype(jnp.float32)
        grad = jnp.where(pre_ref[:, b].reshape(half, LANES) > 0, grad, 0.0)
        ahead, behind = shifted(grad, column, cols)
        for y in range(rows // 2):
            span = slice(y * cols, (y + 1) * cols)
            grad_pad[1, 1 + 2 * y + b] = grad[span].astype(jnp.bfloat16)
            grad_wide[2 * y + b, :, 0:LANES] = ahead[span].astype(jnp.bfloat16)
            grad_wide[2 * y + b, :, LANES : 2 * LANES] = grad[span].astype(jnp.bfloat16)
            grad_wide[2 * y + b, :, 2 * LANES :] = behind[span].astype(jnp.bfloat16)
    grad_halo.send([side for side in SIDES if side[1]])
    near = [(1, 0), (-1, 0)]
    for here in range(2):
        pl.when(core == here)(functools.partial(grad_halo.send, [near[1 - here]]))

    grads = grad_wide[...].reshape(rows * cols, 3 * LANES)
    swaps = []

    def swapped(position):
        kz = PLANES[position]
        swaps[position].wait_recv()
        for tap in range(9):
            total[9 * position + tap] = conv_own[kz, core, tap] + core_in[kz, tap].astype(jnp.float32)

    for position, kz in enumerate(PLANES):
        slab = contract(level_turned[kz], grads, (1, 0))
        for ky in range(3):
            for kx in range(3):
                for part in range(2):
                    top = ky * LANES + part * ROWS
                    block = slab[top : top + ROWS, kx * LANES : (kx + 1) * LANES]
                    conv_own[kz, part, 3 * ky + kx] = block
                    conv_out[kz, part, 3 * ky + kx] = block.astype(jnp.bfloat16)
        swaps.append(
            remote(conv_out.at[kz, 1 - core], core_in.at[kz], core_sems.at[0, kz], core_sems.at[1, kz], partner)
        )
        swaps[position].start()
        if position:
            swapped(position - 1)
            parts[position - 1].scatter1()
    for here in range(2):
        pl.when(core == here)(functools.partial(grad_halo.send, [near[here]]))
    swapped(2)
    parts[2].scatter1()
    parts[3].scatter1()

    grad_halo.receive()
    loads[5].wait()
    for kz in range(3):
        acc = None
        for ky in range(3):
            cells = grad_pad[2 - kz, pl.ds(2 - ky, rows)].reshape(rows * cols, LANES)
            term = contract(cells, weight_ref[3 * kz + ky], (1, 1))
            acc = term if acc is None else acc + term
        input_sum[...] = acc if kz == 0 else input_sum[...] + acc
    column = lax.broadcasted_iota(jnp.int32, (rows * cols, LANES), 0) & (cols - 1)
    ahead, _ = shifted(input_sum[:, 0:LANES], column, cols)
    _, behind = shifted(input_sum[:, 2 * LANES :], column, cols)
    sums = input_sum[:, LANES : 2 * LANES] + ahead + behind
    input_rows[...] = sums.astype(jnp.bfloat16).reshape(input_rows.shape)

    queue = [parts[i] for i in ORDER]
    for stage in ("scatter2", "exchange3", "gather2", "gather1", "gather_core"):
        for part in queue:
            getattr(part, stage)()
    for part in queue:
        part.finish(result.at[1 - core], dummy)
    for swap in swaps:
        swap.wait_send()
    wait_bytes(messages, deep_sems.at[0])
    wait_bytes(planes, deep_sems.at[2])
    level_halo.wait(0)
    grad_halo.wait(0)


def vmem_output(shape, dtype):
    return pltpu.VMEM(shape, dtype)


def in_vmem(array):
    return pltpu.with_memory_space_constraint(array, pltpu.VMEM)


def in_hbm(array):
    return pltpu.with_memory_space_constraint(array, pltpu.HBM)


def per_device(level_input, pre_activation, conv_weight, down_weight, skip_cotangent, deep_cotangent):
    rows, cols, channels = level_input.shape[1:]
    planes, deep_rows, deep_cols, share = deep_cotangent.shape
    counts = (lax.axis_size("gz"), lax.axis_size("gy"))
    side_z, side_y = grid_sides(counts[0])
    n = {"z": side_z, "y": side_y, "x": counts[1], "c": 2}
    cell_count = rows * cols
    cell_total = counts[0] * counts[1] * cell_count
    scales = (math.sqrt(cell_total), math.sqrt(cell_total // 8))
    deep_cells = deep_rows * deep_cols
    wide = counts[0] * share
    pad = (3, rows + 2, cols, channels)
    scratch = [
        pltpu.VMEM((rows // 2, 2, cols, channels), jnp.bfloat16),
        pltpu.VMEM((9, 3 * channels, channels), jnp.bfloat16),
        pltpu.VMEM((4 * channels, 2 * channels), jnp.bfloat16),
        pltpu.VMEM((rows // 2, 2, cols, channels), jnp.bfloat16),
        pltpu.VMEM((deep_cells, share, planes), jnp.bfloat16),
        pltpu.VMEM((side_y, side_z * share, deep_cells), jnp.bfloat16),
        pltpu.VMEM((wide, wide), jnp.bfloat16),
        pltpu.VMEM((2 * side_y, side_z * share, deep_cells), jnp.bfloat16),
        pltpu.VMEM((side_z, side_y * 2 * share, deep_cells), jnp.bfloat16),
        pltpu.VMEM((side_z, side_y * 2 * share, deep_cells), jnp.bfloat16),
        pltpu.VMEM(pad, jnp.bfloat16),
        pltpu.VMEM(pad, jnp.bfloat16),
        pltpu.VMEM((rows, cols, 3 * channels), jnp.bfloat16),
        pltpu.VMEM((2, 2 * channels, cell_count // 2), jnp.bfloat16),
        pltpu.VMEM((3, 3 * channels, cell_count), jnp.bfloat16),
        pltpu.VMEM((cell_count, 3 * channels), jnp.float32),
        pltpu.VMEM((3, 2, 9, ROWS, LANES), jnp.float32),
        pltpu.VMEM((3, 2, 9, ROWS, LANES), jnp.bfloat16),
        pltpu.VMEM((3, 9, ROWS, LANES), jnp.bfloat16),
        pltpu.VMEM((BLOCKS, ROWS, LANES), jnp.float32),
        pltpu.VMEM((max(part_rows(part, n) for part in PARTS), LANES), jnp.bfloat16),
        pltpu.SemaphoreType.DMA((6,)),
        pltpu.SemaphoreType.DMA((4,)),
        pltpu.SemaphoreType.DMA((2, 2)),
        pltpu.SemaphoreType.DMA((2, 2)),
        pltpu.SemaphoreType.DMA((2, 3)),
    ]
    for part in PARTS:
        scratch += part_scratch(part, n)
    input_rows, result = pl.pallas_call(
        functools.partial(level_kernel, n, counts, scales),
        out_shape=(
            vmem_output((rows, cols, channels), jnp.bfloat16),
            vmem_output((2, BLOCKS, ROWS, LANES), jnp.bfloat16),
        ),
        in_specs=[pl.BlockSpec(memory_space=pltpu.HBM)] * 6,
        out_specs=[pl.BlockSpec(memory_space=pltpu.VMEM)] * 2,
        scratch_shapes=scratch,
        compiler_params=pltpu.CompilerParams(
            collective_id=0, has_side_effects=True, vmem_limit_bytes=50 * 1024 * 1024
        ),
    )(
        in_hbm(level_input.reshape(rows, cols, channels)),
        in_hbm(pre_activation.reshape(rows // 2, 2, cols, channels)),
        in_hbm(conv_weight.reshape(9, 3 * channels, channels)),
        in_hbm(down_weight.reshape(2, 4 * channels, 2 * channels)),
        in_hbm(skip_cotangent.reshape(rows // 2, 2, cols, channels)),
        in_hbm(deep_cotangent.transpose(1, 2, 3, 0).reshape(deep_cells, share, planes)),
    )
    input_grad, conv_grad, down_grad = pl.pallas_call(
        store_kernel,
        out_shape=(
            jax.ShapeDtypeStruct((rows, cols, channels), jnp.bfloat16),
            jax.ShapeDtypeStruct((TAPS, 2, ROWS, LANES), jnp.bfloat16),
            jax.ShapeDtypeStruct((2, 8, ROWS, 2 * LANES), jnp.bfloat16),
        ),
        in_specs=[pl.BlockSpec(memory_space=pltpu.VMEM)] * 2,
        out_specs=[pl.BlockSpec(memory_space=pl.ANY)] * 3,
        scratch_shapes=[pltpu.SemaphoreType.DMA((11,))],
    )(in_vmem(input_rows), in_vmem(result))
    return (
        input_grad.reshape(1, rows, cols, channels),
        conv_grad.reshape(3, 3, 3, channels, channels),
        down_grad.reshape(2, 2, 2, channels, 2 * channels),
    )


def solution(mesh):
    return jax.shard_map(
        per_device,
        mesh=mesh,
        in_specs=(
            P("gz", "gy", None, None),
            P("gz", "gy", None, None),
            P(),
            P(),
            P("gz", "gy", None, None),
            P(None, "gy", None, "gz"),
        ),
        out_specs=(P("gz", "gy", None, None), P(), P()),
        check_vma=False,
    )
```

```python
import functools
import math

import jax
import jax.numpy as jnp
from jax import lax
from jax.experimental import pallas as pl
from jax.experimental.pallas import tpu as pltpu
from jax.sharding import PartitionSpec as P

MESH = pl.DeviceIdType.MESH
TAPS = 27
ROWS = 64
LANES = 128
BLOCKS = 44
CONV = 28
PARTS = (
    ("y", "x", "z", 0, 8),
    ("x", "z", "y", 8, 8),
    ("x", "y", "z", 16, 12),
    ("x", "z", "y", 28, 4),
    ("z", "x", "y", 32, 12),
)
FIRST = (3, 1, 4, 0, 2)
LATER = (3, 4, 0, 1, 2)
PLANES = (1, 0, 2)


def grid_sides(gz):
    side = math.isqrt(gz // 2)
    return side, side


class Place:
    def __init__(self, sizes):
        self.n = sizes
        gz = lax.axis_index("gz")
        self.gz = gz
        self.at = {
            "z": gz // (2 * sizes["y"]),
            "y": (gz // 2) % sizes["y"],
            "c": gz % 2,
            "x": lax.axis_index("gy"),
        }

    def peer(self, **moved):
        at = dict(self.at, **moved)
        return ((at["z"] * self.n["y"] + at["y"]) * 2 + at["c"], at["x"])

    def ahead(self, axis, step):
        return (self.at[axis] + step) % self.n[axis]

    def behind(self, axis, step):
        return (self.at[axis] + (self.n[axis] - step)) % self.n[axis]

    def steps(self, axis):
        count = self.n[axis]
        return sorted(range(1, count), key=lambda d: -min(d, count - d))


def remote(src, dst, send_sem, recv_sem, device):
    return pltpu.make_async_remote_copy(
        src_ref=src,
        dst_ref=dst,
        send_sem=send_sem,
        recv_sem=recv_sem,
        device_id=device,
        device_id_type=MESH,
    )


def wait_bytes(window, sem):
    pltpu.make_async_copy(window, window, sem).wait()


def part_shapes(part, n):
    a1, a2, a3, _, count = part
    rows = ROWS // n["y"]
    cut = count // n["x"]
    piece = (cut, rows, LANES)
    first = (cut, ROWS, LANES) if a1 == "x" else (count, rows, LANES)
    return first, piece


def part_rows(part, n):
    a1, a2, a3, _, count = part
    first, piece = (math.prod(shape) // LANES for shape in part_shapes(part, n))
    stages = (n[a1] - 1) * first + (n[a2] - 1) * piece + (n[a3] - 1) * piece
    return stages + (n[a2] - 1) * piece + (n[a1] - 1) * first + count * ROWS


def part_scratch(part, n):
    a1, a2, a3, _, _ = part
    first, piece = part_shapes(part, n)
    return [
        pltpu.VMEM((n[a1],) + first, jnp.bfloat16),
        pltpu.VMEM((n[a1],) + first, jnp.bfloat16),
        pltpu.VMEM((n[a2],) + piece, jnp.float32),
        pltpu.VMEM((n[a2],) + piece, jnp.bfloat16),
        pltpu.VMEM((n[a2],) + piece, jnp.bfloat16),
        pltpu.VMEM((n[a3],) + piece, jnp.bfloat16),
        pltpu.SemaphoreType.DMA((7,)),
    ]


PART_REFS = 7


class PartSum:
    def __init__(self, part, place, total, result, refs, scales):
        self.a1, self.a2, self.a3, self.start, self.count = part
        self.part = part
        self.place = place
        self.total = total
        self.result = result
        self.out1, self.in1, self.own2, self.out2, self.in2, self.all3, self.sems = refs
        self.rows = ROWS // place.n["y"]
        self.cut = self.count // place.n["x"]
        self.scales = scales

    def send(self, src, dst, stage, **moved):
        remote(src, dst, self.sems.at[6], self.sems.at[stage], self.place.peer(**moved)).start()

    def span(self, ref, axes, where, times=1):
        blocks = pl.ds(self.start, self.count)
        rows = slice(None)
        for axis in axes:
            wide = times if axis == axes[-1] else 1
            if axis == "x":
                blocks = pl.ds(self.start + where["x"] * self.cut, self.cut * wide)
            else:
                rows = pl.ds(pl.multiple_of(where[axis] * self.rows, self.rows), self.rows * wide)
        return ref.at[blocks, rows]

    def scatter1(self):
        place = self.place
        for step in place.steps(self.a1):
            to = place.ahead(self.a1, step)
            self.out1[to] = self.span(self.total, (self.a1,), {self.a1: to})[...].astype(jnp.bfloat16)
            self.send(self.out1.at[to], self.in1.at[place.at[self.a1]], 0, **{self.a1: to})

    def collect(self, held, stage, axis, first):
        place = self.place
        wait_bytes(held.at[pl.ds(0, place.n[axis] - 1)], self.sems.at[stage])
        acc = first
        for step in place.steps(axis):
            acc = acc + held[place.behind(axis, step)].astype(jnp.float32)
        return acc

    def scatter2(self):
        place = self.place
        own = self.span(self.total, (self.a1,), place.at)[...]
        acc = self.collect(self.in1, 0, self.a1, own)
        for to in range(place.n[self.a2]):
            if self.a2 == "x":
                piece = acc[to * self.cut : (to + 1) * self.cut]
            else:
                piece = acc[:, to * self.rows : (to + 1) * self.rows]
            self.own2[to] = piece
            self.out2[to] = piece.astype(jnp.bfloat16)
        for step in place.steps(self.a2):
            to = place.ahead(self.a2, step)
            self.send(self.out2.at[to], self.in2.at[place.at[self.a2]], 1, **{self.a2: to})

    def exchange3(self):
        place = self.place
        me = place.at[self.a3]
        acc = self.collect(self.in2, 1, self.a2, self.own2[place.at[self.a2]])
        self.all3[me] = acc.astype(jnp.bfloat16)
        for step in place.steps(self.a3):
            self.send(self.all3.at[me], self.all3.at[me], 2, **{self.a3: place.ahead(self.a3, step)})

    def gather2(self):
        place = self.place
        wait_bytes(self.all3.at[pl.ds(0, place.n[self.a3] - 1)], self.sems.at[2])
        acc = self.all3[0].astype(jnp.float32)
        for source in range(1, place.n[self.a3]):
            acc = acc + self.all3[source].astype(jnp.float32)
        mine = self.span(self.result, (self.a1, self.a2), place.at)
        conv_scale, down_scale = self.scales
        scale = down_scale if self.start >= CONV else conv_scale
        mine[...] = (acc / scale).astype(jnp.bfloat16)
        for step in place.steps(self.a2):
            self.send(mine, mine, 3, **{self.a2: place.ahead(self.a2, step)})

    def gather1(self):
        place = self.place
        zero = dict(place.at, **{self.a2: 0})
        wait_bytes(self.span(self.result, (self.a1, self.a2), zero, place.n[self.a2] - 1), self.sems.at[3])
        mine = self.span(self.result, (self.a1,), place.at)
        for step in place.steps(self.a1):
            self.send(mine, mine, 4, **{self.a1: place.ahead(self.a1, step)})
        self.send(mine, mine, 5, c=1 - place.at["c"])

    def gather_core(self):
        place = self.place
        wait_bytes(self.span(self.result, (self.a1,), {self.a1: 0}, place.n[self.a1] - 1), self.sems.at[4])
        for step in place.steps(self.a1):
            ref = self.span(self.result, (self.a1,), {self.a1: place.behind(self.a1, step)})
            self.send(ref, ref, 5, c=1 - place.at["c"])

    def finish(self, other, dummy):
        wait_bytes(other.at[pl.ds(self.start, self.count)], self.sems.at[5])
        wait_bytes(dummy.at[pl.ds(0, part_rows(self.part, self.place.n))], self.sems.at[6])


def store_kernel(rows_ref, result, input_out, conv_out, down_out, sems):
    copies = [pltpu.make_async_copy(rows_ref, input_out, sems.at[0])]
    for core in range(2):
        for place, kz in enumerate(PLANES):
            source = result.at[core, pl.ds(9 * place, 9)]
            copies.append(
                pltpu.make_async_copy(source, conv_out.at[pl.ds(9 * kz, 9), core], sems.at[len(copies)])
            )
        for side in range(2):
            source = result.at[core, pl.ds(CONV + 8 * side, 8)]
            target = down_out.at[core, :, :, pl.ds(LANES * side, LANES)]
            copies.append(pltpu.make_async_copy(source, target, sems.at[len(copies)]))
    for copy in copies:
        copy.start()
    for copy in copies:
        copy.wait()


SIDES = [(dz, dy) for dz in (1, -1, 0) for dy in (0, 1, -1) if (dz, dy) != (0, 0)]


class Halo:
    def __init__(self, place, counts, padded, sems):
        self.place, self.counts, self.padded, self.sems = place, counts, padded, sems
        self.depth = padded.shape[1] - 2

    def neighbour(self, dz, dy):
        z, y = self.counts
        return ((self.place.gz + dz + z) % z, (self.place.at["x"] + dy + y) % y)

    def send(self, sides):
        own = self.padded.at[1, pl.ds(1, self.depth)]
        for dz, dy in sides:
            if dy == 0:
                src, dst = own, self.padded.at[1 - dz, pl.ds(1, self.depth)]
            elif dy == 1:
                src, dst = own.at[pl.ds(self.depth - 1, 1)], self.padded.at[1 - dz, pl.ds(0, 1)]
            else:
                src, dst = own.at[pl.ds(0, 1)], self.padded.at[1 - dz, pl.ds(self.depth + 1, 1)]
            kind = 0 if dy == 0 else 1
            remote(src, dst, self.sems.at[0, kind], self.sems.at[1, kind], self.neighbour(dz, dy)).start()

    def wait(self, way):
        wait_bytes(self.padded.at[pl.ds(0, 2), pl.ds(0, self.depth)], self.sems.at[way, 0])
        wait_bytes(self.padded.at[pl.ds(0, 3), pl.ds(0, 2)], self.sems.at[way, 1])

    def receive(self):
        self.wait(1)
        z, y = self.place.gz, self.place.at["x"]
        everything = slice(None)
        for edge, window in (
            (z == 0, (0, everything)),
            (z == self.counts[0] - 1, (2, everything)),
            (y == 0, (everything, 0)),
            (y == self.counts[1] - 1, (everything, self.depth + 1)),
        ):

            @pl.when(edge)
            def _():
                rows = self.padded.at[window]
                rows[...] = jnp.zeros(rows.shape, rows.dtype)


def contract(a, b, dims):
    return lax.dot_general(a, b, ((dims[:1], dims[1:]), ((), ())), preferred_element_type=jnp.float32)


def shifted(values, column, count):
    size = values.shape[0]
    ahead = jnp.where(column == count - 1, 0.0, pltpu.roll(values, size - 1, 0))
    behind = jnp.where(column == 0, 0.0, pltpu.roll(values, 1, 0))
    return ahead, behind


def bits(value, start, width):
    return lax.shift_right_logical(value, start) & ((1 << width) - 1)


def level_kernel(
    n,
    counts,
    scales,
    level_hbm,
    pre_hbm,
    weight_hbm,
    down_hbm,
    skip_hbm,
    deep_hbm,
    input_rows,
    result,
    pre_ref,
    weight_ref,
    down_ref,
    skip_ref,
    deep_ref,
    deep_out,
    order,
    deep_in,
    deep_sorted,
    deep_all,
    level_pad,
    grad_pad,
    grad_wide,
    hidden_turned,
    level_turned,
    input_sum,
    conv_own,
    conv_out,
    core_in,
    total,
    dummy,
    load_sems,
    deep_sems,
    level_sems,
    grad_sems,
    core_sems,
    *refs,
):
    place = Place(n)
    core = place.at["c"]
    partner = place.peer(c=1 - core)
    rows, cols = level_hbm.shape[0], level_hbm.shape[1]
    half = rows // 2 * cols
    level_halo = Halo(place, counts, level_pad, level_sems)
    grad_halo = Halo(place, counts, grad_pad, grad_sems)

    level_ref = level_pad.at[1, pl.ds(1, rows)]
    loads = []
    for i, (source, target) in enumerate(
        (
            (deep_hbm, deep_ref),
            (level_hbm, level_ref),
            (down_hbm.at[core], down_ref),
            (pre_hbm, pre_ref),
            (skip_hbm, skip_ref),
            (weight_hbm, weight_ref),
        )
    ):
        loads.append(pltpu.make_async_copy(source, target, load_sems.at[i]))

    loads[0].start()
    barrier = pltpu.get_barrier_semaphore()
    peers = []
    for step in place.steps("y"):
        peers += [place.peer(y=place.ahead("y", step)), place.peer(y=place.ahead("y", step), c=1 - core)]
    peers.append(partner)
    for axis in "zx":
        peers += [place.peer(**{axis: place.ahead(axis, step)}) for step in place.steps(axis)]
    peers += [level_halo.neighbour(dz, dy) for dz, dy in SIDES if dz]
    for device in peers:
        pl.semaphore_signal(barrier, inc=1, device_id=device, device_id_type=MESH)
    for load in loads[1:]:
        load.start()

    wide = order.shape[0]
    share, deep_planes = deep_ref.shape[1], deep_ref.shape[2]
    share_bits = share.bit_length() - 1
    y_bits, z_bits = n["y"].bit_length() - 1, n["z"].bit_length() - 1
    me_y, me_z = place.at["y"], place.at["z"]

    message = lax.broadcasted_iota(jnp.int32, (deep_planes * share, deep_planes), 0)
    plane = lax.broadcasted_iota(jnp.int32, (deep_planes * share, deep_planes), 1)
    plane_of = (bits(message, share_bits, z_bits) << y_bits) + bits(message, share_bits + z_bits, y_bits)
    channel_of = bits(message, 0, share_bits)
    loads[0].wait()
    cells = deep_ref[...].astype(jnp.float32)
    packed = None
    for channel in range(share):
        chosen = jnp.where((plane == plane_of) & (channel_of == channel), 1.0, 0.0).astype(jnp.bfloat16)
        term = contract(chosen, cells[:, channel].astype(jnp.bfloat16), (1, 1))
        packed = term if packed is None else packed + term
    deep_out[...] = packed.astype(jnp.bfloat16).reshape(deep_out.shape)
    deep_in[2 * me_y + core] = deep_out[me_y]
    pl.semaphore_wait(barrier, len(peers))

    for step in place.steps("y") + [0]:
        to = place.ahead("y", step)
        for there in (core, 1 - core) if step else (1 - core,):
            remote(
                deep_out.at[to], deep_in.at[2 * me_y + core], deep_sems.at[0], deep_sems.at[1], place.peer(y=to, c=there)
            ).start()
    loads[1].wait()
    level_halo.send(SIDES)
    row = lax.broadcasted_iota(jnp.int32, (wide, wide), 0)
    col = lax.broadcasted_iota(jnp.int32, (wide, wide), 1)
    low = bits(row, 0, share_bits)
    source = bits(row, share_bits, 1 + y_bits)
    target = bits(row, share_bits + 1 + y_bits, z_bits)
    wanted = ((source << z_bits) + target << share_bits) + low
    order[...] = jnp.where(col == wanted, 1.0, 0.0).astype(jnp.bfloat16)
    total[CONV - 1] = jnp.zeros((ROWS, LANES), jnp.float32)
    messages = deep_in.at[pl.ds(0, 2 * n["y"] - 1)]
    wait_bytes(messages, deep_sems.at[1])
    held = deep_in[...].reshape(wide, half // 2)
    deep_sorted[...] = contract(order[...], held, (1, 0)).astype(jnp.bfloat16).reshape(deep_sorted.shape)
    for step in place.steps("z"):
        to = place.ahead("z", step)
        remote(deep_sorted.at[to], deep_all.at[me_z], deep_sems.at[2], deep_sems.at[3], place.peer(z=to)).start()
    deep_all[me_z] = deep_sorted[me_z]

    column = lax.broadcasted_iota(jnp.int32, (half, LANES), 0) & (cols - 1)
    odd = (column & 1) == 1
    loads[3].wait()
    for b in range(2):
        hidden = jnp.maximum(pre_ref[:, b].reshape(half, LANES).astype(jnp.float32), 0.0)
        for c in range(2):
            chosen = jnp.where(odd, hidden, 0.0) if c else jnp.where(odd, 0.0, hidden)
            hidden_turned[b, pl.ds(c * LANES, LANES)] = chosen.astype(jnp.bfloat16).T
    level_halo.receive()
    for kz in PLANES:
        for ky in range(3):
            cells = level_pad[kz, pl.ds(ky, rows)].reshape(rows * cols, LANES)
            level_turned[kz, pl.ds(ky * LANES, LANES)] = cells.T
    planes = deep_all.at[pl.ds(0, n["z"] - 1)]
    wait_bytes(planes, deep_sems.at[3])

    cell = lax.broadcasted_iota(jnp.int32, (half, half // 2), 0)
    deep_cell = lax.broadcasted_iota(jnp.int32, (half, half // 2), 1)
    spread = jnp.where(lax.shift_right_logical(cell, 1) == deep_cell, 1.0, 0.0).astype(jnp.bfloat16)
    deep = deep_all[...].reshape(wide, half // 2)
    covering = contract(spread, deep, (1, 1)).astype(jnp.bfloat16)
    for b in range(2):
        slab = contract(hidden_turned[b], covering, (1, 0))
        for c in range(2):
            for part in range(2):
                for side in range(2):
                    total[CONV + 8 * side + 2 * (2 * b + c) + part] = slab[
                        c * LANES + part * ROWS : c * LANES + (part + 1) * ROWS, side * LANES : (side + 1) * LANES
                    ]

    parts = []
    for i, part in enumerate(PARTS):
        parts.append(PartSum(part, place, total, result.at[core], refs[i * PART_REFS : (i + 1) * PART_REFS], scales))
    parts[4].scatter1()
    parts[3].scatter1()

    loads[2].wait()
    loads[4].wait()
    down = contract(covering, down_ref[...], (1, 1))
    for b in range(2):
        even_part = down[:, 2 * b * LANES : (2 * b + 1) * LANES]
        odd_part = down[:, (2 * b + 1) * LANES : (2 * b + 2) * LANES]
        grad = jnp.where(odd, odd_part, even_part) + skip_ref[:, b].reshape(half, LANES).astype(jnp.float32)
        grad = jnp.where(pre_ref[:, b].reshape(half, LANES) > 0, grad, 0.0)
        ahead, behind = shifted(grad, column, cols)
        for y in range(rows // 2):
            span = slice(y * cols, (y + 1) * cols)
            grad_pad[1, 1 + 2 * y + b] = grad[span].astype(jnp.bfloat16)
            grad_wide[2 * y + b, :, 0:LANES] = ahead[span].astype(jnp.bfloat16)
            grad_wide[2 * y + b, :, LANES : 2 * LANES] = grad[span].astype(jnp.bfloat16)
            grad_wide[2 * y + b, :, 2 * LANES :] = behind[span].astype(jnp.bfloat16)
    grad_halo.send([side for side in SIDES if side[1]])
    near = [(1, 0), (-1, 0)]
    for here in range(2):
        pl.when(core == here)(functools.partial(grad_halo.send, [near[1 - here]]))

    grads = grad_wide[...].reshape(rows * cols, 3 * LANES)
    swaps = []

    def swapped(position):
        kz = PLANES[position]
        swaps[position].wait_recv()
        for tap in range(9):
            total[9 * position + tap] = conv_own[kz, core, tap] + core_in[kz, tap].astype(jnp.float32)

    for position, kz in enumerate(PLANES):
        slab = contract(level_turned[kz], grads, (1, 0))
        for ky in range(3):
            for kx in range(3):
                for part in range(2):
                    top = ky * LANES + part * ROWS
                    block = slab[top : top + ROWS, kx * LANES : (kx + 1) * LANES]
                    conv_own[kz, part, 3 * ky + kx] = block
                    conv_out[kz, part, 3 * ky + kx] = block.astype(jnp.bfloat16)
        swaps.append(
            remote(conv_out.at[kz, 1 - core], core_in.at[kz], core_sems.at[0, kz], core_sems.at[1, kz], partner)
        )
        swaps[position].start()
        if position:
            swapped(position - 1)
            parts[position - 1].scatter1()
    for here in range(2):
        pl.when(core == here)(functools.partial(grad_halo.send, [near[here]]))
    swapped(2)
    parts[2].scatter1()

    for i in FIRST:
        parts[i].scatter2()

    grad_halo.receive()
    loads[5].wait()
    for kz in range(3):
        acc = None
        for ky in range(3):
            cells = grad_pad[2 - kz, pl.ds(2 - ky, rows)].reshape(rows * cols, LANES)
            term = contract(cells, weight_ref[3 * kz + ky], (1, 1))
            acc = term if acc is None else acc + term
        input_sum[...] = acc if kz == 0 else input_sum[...] + acc
    column = lax.broadcasted_iota(jnp.int32, (rows * cols, LANES), 0) & (cols - 1)
    ahead, _ = shifted(input_sum[:, 0:LANES], column, cols)
    _, behind = shifted(input_sum[:, 2 * LANES :], column, cols)
    sums = input_sum[:, LANES : 2 * LANES] + ahead + behind
    input_rows[...] = sums.astype(jnp.bfloat16).reshape(input_rows.shape)

    queue = [parts[i] for i in LATER]
    for stage in ("exchange3", "gather2", "gather1", "gather_core"):
        for part in queue:
            getattr(part, stage)()
    for part in queue:
        part.finish(result.at[1 - core], dummy)
    for swap in swaps:
        swap.wait_send()
    wait_bytes(messages, deep_sems.at[0])
    wait_bytes(planes, deep_sems.at[2])
    level_halo.wait(0)
    grad_halo.wait(0)


def vmem_output(shape, dtype):
    return pltpu.VMEM(shape, dtype)


def in_vmem(array):
    return pltpu.with_memory_space_constraint(array, pltpu.VMEM)


def in_hbm(array):
    return pltpu.with_memory_space_constraint(array, pltpu.HBM)


def per_device(level_input, pre_activation, conv_weight, down_weight, skip_cotangent, deep_cotangent):
    rows, cols, channels = level_input.shape[1:]
    planes, deep_rows, deep_cols, share = deep_cotangent.shape
    counts = (lax.axis_size("gz"), lax.axis_size("gy"))
    side_z, side_y = grid_sides(counts[0])
    n = {"z": side_z, "y": side_y, "x": counts[1], "c": 2}
    cell_count = rows * cols
    cell_total = counts[0] * counts[1] * cell_count
    scales = (math.sqrt(cell_total), math.sqrt(cell_total // 8))
    deep_cells = deep_rows * deep_cols
    wide = counts[0] * share
    pad = (3, rows + 2, cols, channels)
    scratch = [
        pltpu.VMEM((rows // 2, 2, cols, channels), jnp.bfloat16),
        pltpu.VMEM((9, 3 * channels, channels), jnp.bfloat16),
        pltpu.VMEM((4 * channels, 2 * channels), jnp.bfloat16),
        pltpu.VMEM((rows // 2, 2, cols, channels), jnp.bfloat16),
        pltpu.VMEM((deep_cells, share, planes), jnp.bfloat16),
        pltpu.VMEM((side_y, side_z * share, deep_cells), jnp.bfloat16),
        pltpu.VMEM((wide, wide), jnp.bfloat16),
        pltpu.VMEM((2 * side_y, side_z * share, deep_cells), jnp.bfloat16),
        pltpu.VMEM((side_z, side_y * 2 * share, deep_cells), jnp.bfloat16),
        pltpu.VMEM((side_z, side_y * 2 * share, deep_cells), jnp.bfloat16),
        pltpu.VMEM(pad, jnp.bfloat16),
        pltpu.VMEM(pad, jnp.bfloat16),
        pltpu.VMEM((rows, cols, 3 * channels), jnp.bfloat16),
        pltpu.VMEM((2, 2 * channels, cell_count // 2), jnp.bfloat16),
        pltpu.VMEM((3, 3 * channels, cell_count), jnp.bfloat16),
        pltpu.VMEM((cell_count, 3 * channels), jnp.float32),
        pltpu.VMEM((3, 2, 9, ROWS, LANES), jnp.float32),
        pltpu.VMEM((3, 2, 9, ROWS, LANES), jnp.bfloat16),
        pltpu.VMEM((3, 9, ROWS, LANES), jnp.bfloat16),
        pltpu.VMEM((BLOCKS, ROWS, LANES), jnp.float32),
        pltpu.VMEM((max(part_rows(part, n) for part in PARTS), LANES), jnp.bfloat16),
        pltpu.SemaphoreType.DMA((6,)),
        pltpu.SemaphoreType.DMA((4,)),
        pltpu.SemaphoreType.DMA((2, 2)),
        pltpu.SemaphoreType.DMA((2, 2)),
        pltpu.SemaphoreType.DMA((2, 3)),
    ]
    for part in PARTS:
        scratch += part_scratch(part, n)
    input_rows, result = pl.pallas_call(
        functools.partial(level_kernel, n, counts, scales),
        out_shape=(
            vmem_output((rows, cols, channels), jnp.bfloat16),
            vmem_output((2, BLOCKS, ROWS, LANES), jnp.bfloat16),
        ),
        in_specs=[pl.BlockSpec(memory_space=pltpu.HBM)] * 6,
        out_specs=[pl.BlockSpec(memory_space=pltpu.VMEM)] * 2,
        scratch_shapes=scratch,
        compiler_params=pltpu.CompilerParams(
            collective_id=0, has_side_effects=True, vmem_limit_bytes=50 * 1024 * 1024
        ),
    )(
        in_hbm(level_input.reshape(rows, cols, channels)),
        in_hbm(pre_activation.reshape(rows // 2, 2, cols, channels)),
        in_hbm(conv_weight.reshape(9, 3 * channels, channels)),
        in_hbm(down_weight.reshape(2, 4 * channels, 2 * channels)),
        in_hbm(skip_cotangent.reshape(rows // 2, 2, cols, channels)),
        in_hbm(deep_cotangent.transpose(1, 2, 3, 0).reshape(deep_cells, share, planes)),
    )
    input_grad, conv_grad, down_grad = pl.pallas_call(
        store_kernel,
        out_shape=(
            jax.ShapeDtypeStruct((rows, cols, channels), jnp.bfloat16),
            jax.ShapeDtypeStruct((TAPS, 2, ROWS, LANES), jnp.bfloat16),
            jax.ShapeDtypeStruct((2, 8, ROWS, 2 * LANES), jnp.bfloat16),
        ),
        in_specs=[pl.BlockSpec(memory_space=pltpu.VMEM)] * 2,
        out_specs=[pl.BlockSpec(memory_space=pl.ANY)] * 3,
        scratch_shapes=[pltpu.SemaphoreType.DMA((11,))],
    )(in_vmem(input_rows), in_vmem(result))
    return (
        input_grad.reshape(1, rows, cols, channels),
        conv_grad.reshape(3, 3, 3, channels, channels),
        down_grad.reshape(2, 2, 2, channels, 2 * channels),
    )


def solution(mesh):
    return jax.shard_map(
        per_device,
        mesh=mesh,
        in_specs=(
            P("gz", "gy", None, None),
            P("gz", "gy", None, None),
            P(),
            P(),
            P("gz", "gy", None, None),
            P(None, "gy", None, "gz"),
        ),
        out_specs=(P("gz", "gy", None, None), P(), P()),
        check_vma=False,
    )
```

```python
import functools
import math

import jax
import jax.numpy as jnp
from jax import lax
from jax.experimental import pallas as pl
from jax.experimental.pallas import tpu as pltpu
from jax.sharding import PartitionSpec as P

MESH = pl.DeviceIdType.MESH
TAPS = 27
ROWS = 64
LANES = 128
BLOCKS = 44
CONV = 28
PARTS = (
    ("y", "x", "z", 0, 8),
    ("x", "z", "y", 8, 8),
    ("x", "y", "z", 16, 12),
    ("x", "z", "y", 28, 4),
    ("z", "x", "y", 32, 12),
)
STAGES = (
    ("exchange3", (3, 0, 1, 4, 2)),
    ("gather2", (3, 0, 1, 4, 2)),
    ("gather1", (3, 0, 4, 1, 2)),
    ("gather_core", (3, 0, 1, 4, 2)),
)
PLANES = (1, 0, 2)


def grid_sides(gz):
    side = math.isqrt(gz // 2)
    return side, side


class Place:
    def __init__(self, sizes):
        self.n = sizes
        gz = lax.axis_index("gz")
        self.gz = gz
        self.at = {
            "z": gz // (2 * sizes["y"]),
            "y": (gz // 2) % sizes["y"],
            "c": gz % 2,
            "x": lax.axis_index("gy"),
        }

    def peer(self, **moved):
        at = dict(self.at, **moved)
        return ((at["z"] * self.n["y"] + at["y"]) * 2 + at["c"], at["x"])

    def ahead(self, axis, step):
        return (self.at[axis] + step) % self.n[axis]

    def behind(self, axis, step):
        return (self.at[axis] + (self.n[axis] - step)) % self.n[axis]

    def steps(self, axis):
        count = self.n[axis]
        return sorted(range(1, count), key=lambda d: -min(d, count - d))


def remote(src, dst, send_sem, recv_sem, device):
    return pltpu.make_async_remote_copy(
        src_ref=src,
        dst_ref=dst,
        send_sem=send_sem,
        recv_sem=recv_sem,
        device_id=device,
        device_id_type=MESH,
    )


def wait_bytes(window, sem):
    pltpu.make_async_copy(window, window, sem).wait()


def part_shapes(part, n):
    a1, a2, a3, _, count = part
    rows = ROWS // n["y"]
    cut = count // n["x"]
    piece = (cut, rows, LANES)
    first = (cut, ROWS, LANES) if a1 == "x" else (count, rows, LANES)
    return first, piece


def part_rows(part, n):
    a1, a2, a3, _, count = part
    first, piece = (math.prod(shape) // LANES for shape in part_shapes(part, n))
    stages = (n[a1] - 1) * first + (n[a2] - 1) * piece + (n[a3] - 1) * piece
    return stages + (n[a2] - 1) * piece + (n[a1] - 1) * first + count * ROWS


def part_scratch(part, n):
    a1, a2, a3, _, _ = part
    first, piece = part_shapes(part, n)
    return [
        pltpu.VMEM((n[a1],) + first, jnp.bfloat16),
        pltpu.VMEM((n[a1],) + first, jnp.bfloat16),
        pltpu.VMEM((n[a2],) + piece, jnp.float32),
        pltpu.VMEM((n[a2],) + piece, jnp.bfloat16),
        pltpu.VMEM((n[a2],) + piece, jnp.bfloat16),
        pltpu.VMEM((n[a3],) + piece, jnp.bfloat16),
        pltpu.SemaphoreType.DMA((7,)),
    ]


PART_REFS = 7


class PartSum:
    def __init__(self, part, place, total, result, refs, scales):
        self.a1, self.a2, self.a3, self.start, self.count = part
        self.part = part
        self.place = place
        self.total = total
        self.result = result
        self.out1, self.in1, self.own2, self.out2, self.in2, self.all3, self.sems = refs
        self.rows = ROWS // place.n["y"]
        self.cut = self.count // place.n["x"]
        self.scales = scales

    def send(self, src, dst, stage, **moved):
        remote(src, dst, self.sems.at[6], self.sems.at[stage], self.place.peer(**moved)).start()

    def span(self, ref, axes, where, times=1):
        blocks = pl.ds(self.start, self.count)
        rows = slice(None)
        for axis in axes:
            wide = times if axis == axes[-1] else 1
            if axis == "x":
                blocks = pl.ds(self.start + where["x"] * self.cut, self.cut * wide)
            else:
                rows = pl.ds(pl.multiple_of(where[axis] * self.rows, self.rows), self.rows * wide)
        return ref.at[blocks, rows]

    def scatter1(self):
        place = self.place
        for step in place.steps(self.a1):
            to = place.ahead(self.a1, step)
            self.out1[to] = self.span(self.total, (self.a1,), {self.a1: to})[...].astype(jnp.bfloat16)
            self.send(self.out1.at[to], self.in1.at[place.at[self.a1]], 0, **{self.a1: to})

    def collect(self, held, stage, axis, first):
        place = self.place
        wait_bytes(held.at[pl.ds(0, place.n[axis] - 1)], self.sems.at[stage])
        acc = first
        for step in place.steps(axis):
            acc = acc + held[place.behind(axis, step)].astype(jnp.float32)
        return acc

    def scatter2(self):
        place = self.place
        own = self.span(self.total, (self.a1,), place.at)[...]
        acc = self.collect(self.in1, 0, self.a1, own)
        for to in range(place.n[self.a2]):
            if self.a2 == "x":
                piece = acc[to * self.cut : (to + 1) * self.cut]
            else:
                piece = acc[:, to * self.rows : (to + 1) * self.rows]
            self.own2[to] = piece
            self.out2[to] = piece.astype(jnp.bfloat16)
        for step in place.steps(self.a2):
            to = place.ahead(self.a2, step)
            self.send(self.out2.at[to], self.in2.at[place.at[self.a2]], 1, **{self.a2: to})

    def exchange3(self):
        place = self.place
        me = place.at[self.a3]
        acc = self.collect(self.in2, 1, self.a2, self.own2[place.at[self.a2]])
        self.all3[me] = acc.astype(jnp.bfloat16)
        for step in place.steps(self.a3):
            self.send(self.all3.at[me], self.all3.at[me], 2, **{self.a3: place.ahead(self.a3, step)})

    def gather2(self):
        place = self.place
        wait_bytes(self.all3.at[pl.ds(0, place.n[self.a3] - 1)], self.sems.at[2])
        acc = self.all3[0].astype(jnp.float32)
        for source in range(1, place.n[self.a3]):
            acc = acc + self.all3[source].astype(jnp.float32)
        mine = self.span(self.result, (self.a1, self.a2), place.at)
        conv_scale, down_scale = self.scales
        scale = down_scale if self.start >= CONV else conv_scale
        mine[...] = (acc / scale).astype(jnp.bfloat16)
        for step in place.steps(self.a2):
            self.send(mine, mine, 3, **{self.a2: place.ahead(self.a2, step)})

    def gather1(self):
        place = self.place
        zero = dict(place.at, **{self.a2: 0})
        wait_bytes(self.span(self.result, (self.a1, self.a2), zero, place.n[self.a2] - 1), self.sems.at[3])
        mine = self.span(self.result, (self.a1,), place.at)
        for step in place.steps(self.a1):
            self.send(mine, mine, 4, **{self.a1: place.ahead(self.a1, step)})
        self.send(mine, mine, 5, c=1 - place.at["c"])

    def gather_core(self):
        place = self.place
        wait_bytes(self.span(self.result, (self.a1,), {self.a1: 0}, place.n[self.a1] - 1), self.sems.at[4])
        for step in place.steps(self.a1):
            ref = self.span(self.result, (self.a1,), {self.a1: place.behind(self.a1, step)})
            self.send(ref, ref, 5, c=1 - place.at["c"])

    def finish(self, other, dummy):
        wait_bytes(other.at[pl.ds(self.start, self.count)], self.sems.at[5])
        wait_bytes(dummy.at[pl.ds(0, part_rows(self.part, self.place.n))], self.sems.at[6])


def store_kernel(rows_ref, result, input_out, conv_out, down_out, sems):
    copies = [pltpu.make_async_copy(rows_ref, input_out, sems.at[0])]
    for core in range(2):
        for place, kz in enumerate(PLANES):
            source = result.at[core, pl.ds(9 * place, 9)]
            copies.append(
                pltpu.make_async_copy(source, conv_out.at[pl.ds(9 * kz, 9), core], sems.at[len(copies)])
            )
        for side in range(2):
            source = result.at[core, pl.ds(CONV + 8 * side, 8)]
            target = down_out.at[core, :, :, pl.ds(LANES * side, LANES)]
            copies.append(pltpu.make_async_copy(source, target, sems.at[len(copies)]))
    for copy in copies:
        copy.start()
    for copy in copies:
        copy.wait()


SIDES = [(dz, dy) for dz in (1, -1, 0) for dy in (0, 1, -1) if (dz, dy) != (0, 0)]


class Halo:
    def __init__(self, place, counts, padded, sems):
        self.place, self.counts, self.padded, self.sems = place, counts, padded, sems
        self.depth = padded.shape[1] - 2

    def neighbour(self, dz, dy):
        z, y = self.counts
        return ((self.place.gz + dz + z) % z, (self.place.at["x"] + dy + y) % y)

    def send(self, sides):
        own = self.padded.at[1, pl.ds(1, self.depth)]
        for dz, dy in sides:
            if dy == 0:
                src, dst = own, self.padded.at[1 - dz, pl.ds(1, self.depth)]
            elif dy == 1:
                src, dst = own.at[pl.ds(self.depth - 1, 1)], self.padded.at[1 - dz, pl.ds(0, 1)]
            else:
                src, dst = own.at[pl.ds(0, 1)], self.padded.at[1 - dz, pl.ds(self.depth + 1, 1)]
            kind = 0 if dy == 0 else 1
            remote(src, dst, self.sems.at[0, kind], self.sems.at[1, kind], self.neighbour(dz, dy)).start()

    def wait(self, way):
        wait_bytes(self.padded.at[pl.ds(0, 2), pl.ds(0, self.depth)], self.sems.at[way, 0])
        wait_bytes(self.padded.at[pl.ds(0, 3), pl.ds(0, 2)], self.sems.at[way, 1])

    def receive(self):
        self.wait(1)
        z, y = self.place.gz, self.place.at["x"]
        everything = slice(None)
        for edge, window in (
            (z == 0, (0, everything)),
            (z == self.counts[0] - 1, (2, everything)),
            (y == 0, (everything, 0)),
            (y == self.counts[1] - 1, (everything, self.depth + 1)),
        ):

            @pl.when(edge)
            def _():
                rows = self.padded.at[window]
                rows[...] = jnp.zeros(rows.shape, rows.dtype)


def contract(a, b, dims):
    return lax.dot_general(a, b, ((dims[:1], dims[1:]), ((), ())), preferred_element_type=jnp.float32)


def shifted(values, column, count):
    size = values.shape[0]
    ahead = jnp.where(column == count - 1, 0.0, pltpu.roll(values, size - 1, 0))
    behind = jnp.where(column == 0, 0.0, pltpu.roll(values, 1, 0))
    return ahead, behind


def bits(value, start, width):
    return lax.shift_right_logical(value, start) & ((1 << width) - 1)


def level_kernel(
    n,
    counts,
    scales,
    level_hbm,
    pre_hbm,
    weight_hbm,
    down_hbm,
    skip_hbm,
    deep_hbm,
    input_rows,
    result,
    pre_ref,
    weight_ref,
    down_ref,
    skip_ref,
    deep_ref,
    deep_out,
    order,
    deep_in,
    deep_sorted,
    deep_all,
    level_pad,
    grad_pad,
    grad_wide,
    hidden_turned,
    level_turned,
    input_sum,
    conv_own,
    conv_out,
    core_in,
    total,
    dummy,
    load_sems,
    deep_sems,
    level_sems,
    grad_sems,
    core_sems,
    *refs,
):
    place = Place(n)
    core = place.at["c"]
    partner = place.peer(c=1 - core)
    rows, cols = level_hbm.shape[0], level_hbm.shape[1]
    half = rows // 2 * cols
    level_halo = Halo(place, counts, level_pad, level_sems)
    grad_halo = Halo(place, counts, grad_pad, grad_sems)

    level_ref = level_pad.at[1, pl.ds(1, rows)]
    loads = []
    for i, (source, target) in enumerate(
        (
            (deep_hbm, deep_ref),
            (level_hbm, level_ref),
            (down_hbm.at[core], down_ref),
            (pre_hbm, pre_ref),
            (skip_hbm, skip_ref),
            (weight_hbm, weight_ref),
        )
    ):
        loads.append(pltpu.make_async_copy(source, target, load_sems.at[i]))

    loads[0].start()
    barrier = pltpu.get_barrier_semaphore()
    peers = []
    for step in place.steps("y"):
        peers += [place.peer(y=place.ahead("y", step)), place.peer(y=place.ahead("y", step), c=1 - core)]
    peers.append(partner)
    for axis in "zx":
        peers += [place.peer(**{axis: place.ahead(axis, step)}) for step in place.steps(axis)]
    peers += [level_halo.neighbour(dz, dy) for dz, dy in SIDES if dz]
    for device in peers:
        pl.semaphore_signal(barrier, inc=1, device_id=device, device_id_type=MESH)
    for load in loads[1:]:
        load.start()

    wide = order.shape[0]
    share, deep_planes = deep_ref.shape[1], deep_ref.shape[2]
    share_bits = share.bit_length() - 1
    y_bits, z_bits = n["y"].bit_length() - 1, n["z"].bit_length() - 1
    me_y, me_z = place.at["y"], place.at["z"]

    message = lax.broadcasted_iota(jnp.int32, (deep_planes * share, deep_planes), 0)
    plane = lax.broadcasted_iota(jnp.int32, (deep_planes * share, deep_planes), 1)
    plane_of = (bits(message, share_bits, z_bits) << y_bits) + bits(message, share_bits + z_bits, y_bits)
    channel_of = bits(message, 0, share_bits)
    loads[0].wait()
    cells = deep_ref[...].astype(jnp.float32)
    packed = None
    for channel in range(share):
        chosen = jnp.where((plane == plane_of) & (channel_of == channel), 1.0, 0.0).astype(jnp.bfloat16)
        term = contract(chosen, cells[:, channel].astype(jnp.bfloat16), (1, 1))
        packed = term if packed is None else packed + term
    deep_out[...] = packed.astype(jnp.bfloat16).reshape(deep_out.shape)
    deep_in[2 * me_y + core] = deep_out[me_y]
    pl.semaphore_wait(barrier, len(peers))

    for step in place.steps("y") + [0]:
        to = place.ahead("y", step)
        for there in (core, 1 - core) if step else (1 - core,):
            remote(
                deep_out.at[to], deep_in.at[2 * me_y + core], deep_sems.at[0], deep_sems.at[1], place.peer(y=to, c=there)
            ).start()
    loads[1].wait()
    level_halo.send(SIDES)
    row = lax.broadcasted_iota(jnp.int32, (wide, wide), 0)
    col = lax.broadcasted_iota(jnp.int32, (wide, wide), 1)
    low = bits(row, 0, share_bits)
    source = bits(row, share_bits, 1 + y_bits)
    target = bits(row, share_bits + 1 + y_bits, z_bits)
    wanted = ((source << z_bits) + target << share_bits) + low
    order[...] = jnp.where(col == wanted, 1.0, 0.0).astype(jnp.bfloat16)
    total[CONV - 1] = jnp.zeros((ROWS, LANES), jnp.float32)
    messages = deep_in.at[pl.ds(0, 2 * n["y"] - 1)]
    wait_bytes(messages, deep_sems.at[1])
    held = deep_in[...].reshape(wide, half // 2)
    deep_sorted[...] = contract(order[...], held, (1, 0)).astype(jnp.bfloat16).reshape(deep_sorted.shape)
    for step in place.steps("z"):
        to = place.ahead("z", step)
        remote(deep_sorted.at[to], deep_all.at[me_z], deep_sems.at[2], deep_sems.at[3], place.peer(z=to)).start()
    deep_all[me_z] = deep_sorted[me_z]

    column = lax.broadcasted_iota(jnp.int32, (half, LANES), 0) & (cols - 1)
    odd = (column & 1) == 1
    loads[3].wait()
    for b in range(2):
        hidden = jnp.maximum(pre_ref[:, b].reshape(half, LANES).astype(jnp.float32), 0.0)
        for c in range(2):
            chosen = jnp.where(odd, hidden, 0.0) if c else jnp.where(odd, 0.0, hidden)
            hidden_turned[b, pl.ds(c * LANES, LANES)] = chosen.astype(jnp.bfloat16).T
    level_halo.receive()
    for kz in PLANES:
        for ky in range(3):
            cells = level_pad[kz, pl.ds(ky, rows)].reshape(rows * cols, LANES)
            level_turned[kz, pl.ds(ky * LANES, LANES)] = cells.T
    planes = deep_all.at[pl.ds(0, n["z"] - 1)]
    wait_bytes(planes, deep_sems.at[3])

    cell = lax.broadcasted_iota(jnp.int32, (half, half // 2), 0)
    deep_cell = lax.broadcasted_iota(jnp.int32, (half, half // 2), 1)
    spread = jnp.where(lax.shift_right_logical(cell, 1) == deep_cell, 1.0, 0.0).astype(jnp.bfloat16)
    deep = deep_all[...].reshape(wide, half // 2)
    covering = contract(spread, deep, (1, 1)).astype(jnp.bfloat16)
    for b in range(2):
        slab = contract(hidden_turned[b], covering, (1, 0))
        for c in range(2):
            for part in range(2):
                for side in range(2):
                    total[CONV + 8 * side + 2 * (2 * b + c) + part] = slab[
                        c * LANES + part * ROWS : c * LANES + (part + 1) * ROWS, side * LANES : (side + 1) * LANES
                    ]

    parts = []
    for i, part in enumerate(PARTS):
        parts.append(PartSum(part, place, total, result.at[core], refs[i * PART_REFS : (i + 1) * PART_REFS], scales))
    parts[4].scatter1()
    parts[3].scatter1()

    loads[2].wait()
    loads[4].wait()
    down = contract(covering, down_ref[...], (1, 1))
    for b in range(2):
        even_part = down[:, 2 * b * LANES : (2 * b + 1) * LANES]
        odd_part = down[:, (2 * b + 1) * LANES : (2 * b + 2) * LANES]
        grad = jnp.where(odd, odd_part, even_part) + skip_ref[:, b].reshape(half, LANES).astype(jnp.float32)
        grad = jnp.where(pre_ref[:, b].reshape(half, LANES) > 0, grad, 0.0)
        ahead, behind = shifted(grad, column, cols)
        for y in range(rows // 2):
            span = slice(y * cols, (y + 1) * cols)
            grad_pad[1, 1 + 2 * y + b] = grad[span].astype(jnp.bfloat16)
            grad_wide[2 * y + b, :, 0:LANES] = ahead[span].astype(jnp.bfloat16)
            grad_wide[2 * y + b, :, LANES : 2 * LANES] = grad[span].astype(jnp.bfloat16)
            grad_wide[2 * y + b, :, 2 * LANES :] = behind[span].astype(jnp.bfloat16)
    grad_halo.send([side for side in SIDES if side[1]])
    near = [(1, 0), (-1, 0)]
    for here in range(2):
        pl.when(core == here)(functools.partial(grad_halo.send, [near[1 - here]]))

    grads = grad_wide[...].reshape(rows * cols, 3 * LANES)
    swaps = []

    def swapped(position):
        kz = PLANES[position]
        swaps[position].wait_recv()
        for tap in range(9):
            total[9 * position + tap] = conv_own[kz, core, tap] + core_in[kz, tap].astype(jnp.float32)

    for position, kz in enumerate(PLANES):
        slab = contract(level_turned[kz], grads, (1, 0))
        for ky in range(3):
            for kx in range(3):
                for part in range(2):
                    top = ky * LANES + part * ROWS
                    block = slab[top : top + ROWS, kx * LANES : (kx + 1) * LANES]
                    conv_own[kz, part, 3 * ky + kx] = block
                    conv_out[kz, part, 3 * ky + kx] = block.astype(jnp.bfloat16)
        swaps.append(
            remote(conv_out.at[kz, 1 - core], core_in.at[kz], core_sems.at[0, kz], core_sems.at[1, kz], partner)
        )
        swaps[position].start()
    for position in range(3):
        swapped(position)
        parts[position].scatter1()
    for here in range(2):
        pl.when(core == here)(functools.partial(grad_halo.send, [near[here]]))

    for i in (3, 1, 0, 2, 4):
        parts[i].scatter2()

    grad_halo.receive()
    loads[5].wait()
    for kz in range(3):
        acc = None
        for ky in range(3):
            cells = grad_pad[2 - kz, pl.ds(2 - ky, rows)].reshape(rows * cols, LANES)
            term = contract(cells, weight_ref[3 * kz + ky], (1, 1))
            acc = term if acc is None else acc + term
        input_sum[...] = acc if kz == 0 else input_sum[...] + acc
    column = lax.broadcasted_iota(jnp.int32, (rows * cols, LANES), 0) & (cols - 1)
    ahead, _ = shifted(input_sum[:, 0:LANES], column, cols)
    _, behind = shifted(input_sum[:, 2 * LANES :], column, cols)
    sums = input_sum[:, LANES : 2 * LANES] + ahead + behind
    input_rows[...] = sums.astype(jnp.bfloat16).reshape(input_rows.shape)

    for stage, queue in STAGES:
        for i in queue:
            getattr(parts[i], stage)()
    for part in parts:
        part.finish(result.at[1 - core], dummy)
    for swap in swaps:
        swap.wait_send()
    wait_bytes(messages, deep_sems.at[0])
    wait_bytes(planes, deep_sems.at[2])
    level_halo.wait(0)
    grad_halo.wait(0)


def vmem_output(shape, dtype):
    return pltpu.VMEM(shape, dtype)


def in_vmem(array):
    return pltpu.with_memory_space_constraint(array, pltpu.VMEM)


def in_hbm(array):
    return pltpu.with_memory_space_constraint(array, pltpu.HBM)


def per_device(level_input, pre_activation, conv_weight, down_weight, skip_cotangent, deep_cotangent):
    rows, cols, channels = level_input.shape[1:]
    planes, deep_rows, deep_cols, share = deep_cotangent.shape
    counts = (lax.axis_size("gz"), lax.axis_size("gy"))
    side_z, side_y = grid_sides(counts[0])
    n = {"z": side_z, "y": side_y, "x": counts[1], "c": 2}
    cell_count = rows * cols
    cell_total = counts[0] * counts[1] * cell_count
    scales = (math.sqrt(cell_total), math.sqrt(cell_total // 8))
    deep_cells = deep_rows * deep_cols
    wide = counts[0] * share
    pad = (3, rows + 2, cols, channels)
    scratch = [
        pltpu.VMEM((rows // 2, 2, cols, channels), jnp.bfloat16),
        pltpu.VMEM((9, 3 * channels, channels), jnp.bfloat16),
        pltpu.VMEM((4 * channels, 2 * channels), jnp.bfloat16),
        pltpu.VMEM((rows // 2, 2, cols, channels), jnp.bfloat16),
        pltpu.VMEM((deep_cells, share, planes), jnp.bfloat16),
        pltpu.VMEM((side_y, side_z * share, deep_cells), jnp.bfloat16),
        pltpu.VMEM((wide, wide), jnp.bfloat16),
        pltpu.VMEM((2 * side_y, side_z * share, deep_cells), jnp.bfloat16),
        pltpu.VMEM((side_z, side_y * 2 * share, deep_cells), jnp.bfloat16),
        pltpu.VMEM((side_z, side_y * 2 * share, deep_cells), jnp.bfloat16),
        pltpu.VMEM(pad, jnp.bfloat16),
        pltpu.VMEM(pad, jnp.bfloat16),
        pltpu.VMEM((rows, cols, 3 * channels), jnp.bfloat16),
        pltpu.VMEM((2, 2 * channels, cell_count // 2), jnp.bfloat16),
        pltpu.VMEM((3, 3 * channels, cell_count), jnp.bfloat16),
        pltpu.VMEM((cell_count, 3 * channels), jnp.float32),
        pltpu.VMEM((3, 2, 9, ROWS, LANES), jnp.float32),
        pltpu.VMEM((3, 2, 9, ROWS, LANES), jnp.bfloat16),
        pltpu.VMEM((3, 9, ROWS, LANES), jnp.bfloat16),
        pltpu.VMEM((BLOCKS, ROWS, LANES), jnp.float32),
        pltpu.VMEM((max(part_rows(part, n) for part in PARTS), LANES), jnp.bfloat16),
        pltpu.SemaphoreType.DMA((6,)),
        pltpu.SemaphoreType.DMA((4,)),
        pltpu.SemaphoreType.DMA((2, 2)),
        pltpu.SemaphoreType.DMA((2, 2)),
        pltpu.SemaphoreType.DMA((2, 3)),
    ]
    for part in PARTS:
        scratch += part_scratch(part, n)
    input_rows, result = pl.pallas_call(
        functools.partial(level_kernel, n, counts, scales),
        out_shape=(
            vmem_output((rows, cols, channels), jnp.bfloat16),
            vmem_output((2, BLOCKS, ROWS, LANES), jnp.bfloat16),
        ),
        in_specs=[pl.BlockSpec(memory_space=pltpu.HBM)] * 6,
        out_specs=[pl.BlockSpec(memory_space=pltpu.VMEM)] * 2,
        scratch_shapes=scratch,
        compiler_params=pltpu.CompilerParams(
            collective_id=0, has_side_effects=True, vmem_limit_bytes=50 * 1024 * 1024
        ),
    )(
        in_hbm(level_input.reshape(rows, cols, channels)),
        in_hbm(pre_activation.reshape(rows // 2, 2, cols, channels)),
        in_hbm(conv_weight.reshape(9, 3 * channels, channels)),
        in_hbm(down_weight.reshape(2, 4 * channels, 2 * channels)),
        in_hbm(skip_cotangent.reshape(rows // 2, 2, cols, channels)),
        in_hbm(deep_cotangent.transpose(1, 2, 3, 0).reshape(deep_cells, share, planes)),
    )
    input_grad, conv_grad, down_grad = pl.pallas_call(
        store_kernel,
        out_shape=(
            jax.ShapeDtypeStruct((rows, cols, channels), jnp.bfloat16),
            jax.ShapeDtypeStruct((TAPS, 2, ROWS, LANES), jnp.bfloat16),
            jax.ShapeDtypeStruct((2, 8, ROWS, 2 * LANES), jnp.bfloat16),
        ),
        in_specs=[pl.BlockSpec(memory_space=pltpu.VMEM)] * 2,
        out_specs=[pl.BlockSpec(memory_space=pl.ANY)] * 3,
        scratch_shapes=[pltpu.SemaphoreType.DMA((11,))],
    )(in_vmem(input_rows), in_vmem(result))
    return (
        input_grad.reshape(1, rows, cols, channels),
        conv_grad.reshape(3, 3, 3, channels, channels),
        down_grad.reshape(2, 2, 2, channels, 2 * channels),
    )


def solution(mesh):
    return jax.shard_map(
        per_device,
        mesh=mesh,
        in_specs=(
            P("gz", "gy", None, None),
            P("gz", "gy", None, None),
            P(),
            P(),
            P("gz", "gy", None, None),
            P(None, "gy", None, "gz"),
        ),
        out_specs=(P("gz", "gy", None, None), P(), P()),
        check_vma=False,
    )
```
